128 devices in a mesh: grp: 4 (over z), slab: 32 (over y, x, core).
Axes of the slice: x: 4, y: 4, z: 4, core: 2. Of those that a mesh axis runs over, the one named last changes fastest.
Arguments:
- tensor: float32 [672, 256, 672], P('grp', 'slab'), may hold values from -20 to 20
- start_one: float32 [672, 96], replicated, may hold values from -6 to 6
- start_two: float32 [672, 96], replicated, may hold values from -6 to 6
Outputs:
- basis_one: float32 [672, 96], replicated
- basis_two: float32 [672, 96], replicated
- core: float32 [96, 256, 96], P('grp', 'slab')
The draws below stay inside these ranges and needn't reach their ends.
All inputs are finite; a program needn't handle non-finite values.
Results may differ from the reference program's by a relative error of at most 0.0003.
Values sent between devices are 32-bit elements; how exact they have to be, the bound alone decides.
A program may use at most 64 MiB of HBM per device.

```python
import jax
import jax.numpy as jnp
from jax import lax

N1 = 672
N2 = 672
RANK1 = 96
RANK2 = 96
ITERS = 2
COLS = 256


def draw_tensor(key, part):
    modes = 2 * RANK1 + RANK1 // 2
    key_power = jax.random.fold_in(key, 11)
    key_second = jax.random.fold_in(key, 23)
    key_columns = jax.random.fold_in(key, 37)
    key_first = jax.random.fold_in(key, 41)
    key_noise = jax.random.fold_in(key, 53)
    key_colscale = jax.random.fold_in(key, 67)
    key_rowscale = jax.random.fold_in(key, 79)
    index = jnp.arange(modes, dtype=jnp.float32)
    strong = index < RANK1
    top_pos = index / max(RANK1 - 1, 1)
    tail_pos = (index - RANK1) / max(modes - RANK1 - 1, 1)
    level = jnp.where(strong, top_pos * jnp.log(0.3), jnp.log(0.1) + tail_pos * jnp.log(0.3))
    jitter = jax.random.uniform(key_power, (modes,), jnp.float32, jnp.log(0.8), jnp.log(1.25))
    power = jnp.exp(level + jitter)
    amplitude = jnp.sqrt(power / jnp.sum(power))
    second = jax.random.normal(key_second, (N2, modes), jnp.float32)
    columns = jax.random.normal(key_columns, (COLS, modes), jnp.float32)
    first = jax.random.normal(key_first, (N1, modes), jnp.float32)
    noise = jax.random.normal(key_noise, (N2, COLS, N1), jnp.float32)
    lowest = jnp.log(0.1)
    mixed = (second * amplitude[None, :])[:, None, :] * columns[None, :, :]
    signal = jnp.dot(mixed.reshape(N2 * COLS, modes), first.T).reshape(N2, COLS, N1)
    scale_columns = jnp.exp(jax.random.uniform(key_colscale, (COLS,), jnp.float32, lowest, 0.0))
    scale_rows = jnp.exp(jax.random.uniform(key_rowscale, (N2,), jnp.float32, jnp.log(0.5), 0.0))
    values = 4.0 * scale_rows[:, None, None] * scale_columns[None, :, None] * (signal + jnp.sqrt(0.3) * noise)
    return jnp.clip(values, -20.0, 20.0).astype(jnp.float32)


def centred(stream_key, dims, width, bound, held_as=jnp.bfloat16):
    values = width * jax.random.normal(stream_key, dims, jnp.float32)
    return jnp.clip(values, min=-bound, max=bound).astype(held_as)


def setup_inputs(seed: int = 0) -> dict:
    seeds = jax.random.split(jax.random.key(seed), 4)
    return {
        "tensor": draw_tensor(jax.random.fold_in(seeds[3], 71), 0),
        "start_one": centred(seeds[1], (N1, RANK1), 1.0, 6.0, jnp.float32),
        "start_two": centred(seeds[2], (N2, RANK2), 1.0, 6.0, jnp.float32),
    }


HIGH = lax.Precision.HIGHEST

def iterate_basis(gram, start):
    current = start
    for _ in range(ITERS):
        widened = jnp.dot(gram, current, precision=HIGH)
        cross = jnp.dot(widened.T, widened, precision=HIGH)
        lower_small = jnp.linalg.cholesky(cross)
        current = lax.linalg.triangular_solve(lower_small, widened, left_side=False, lower=True, transpose_a=True)
    return current

def reference(tensor, start_one, start_two):
    gram_one = jnp.einsum('jmi,jmk->ik', tensor, tensor, precision=HIGH)
    basis_one = iterate_basis(gram_one, start_one)
    reduced = jnp.einsum('jmi,ia->jma', tensor, basis_one, precision=HIGH)
    gram_two = jnp.einsum('jma,kma->jk', reduced, reduced, precision=HIGH)
    basis_two = iterate_basis(gram_two, start_two)
    core = jnp.einsum('jb,jma->bma', basis_two, reduced, precision=HIGH)
    return (basis_one, basis_two, core)
```

```python
import jax
import jax.numpy as jnp
from jax import lax
from jax.experimental import pallas as pl
from jax.experimental.pallas import tpu as pltpu
from jax.sharding import PartitionSpec as P

MESH = pl.DeviceIdType.MESH
F32 = jnp.float32
BF16 = jnp.bfloat16

N = 672
NP = 768
RANK = 96
LANES = 128
GRP = 4
COLS = 8
ROWS = N // GRP
CHUNK = 448
CHUNKS = ROWS * COLS // CHUNK
CHIPS = 64
FOLD = N // 4
NT = (((0,), (0,)), ((), ()))
NN = (((1,), (0,)), ((), ()))
TN = (((1,), (1,)), ((), ()))


def dot(a, b, dims):
    return lax.dot_general(a, b, dims, preferred_element_type=F32)


def split(x):
    high = x.astype(BF16)
    return high, (x - high.astype(F32)).astype(BF16)


def halves(x):
    return x[:, :LANES] + x[:, LANES:]


def tops(x):
    return x[:LANES] + x[LANES:]


def lane(shape):
    return lax.broadcasted_iota(jnp.int32, shape, len(shape) - 1)


def kernel(
    tensor, start_one, start_two, out_one, out_two, out_core,
    staged, high, low, block, width, rhigh, rlow, rtilde, mode, given,
    packed, summed, pair, gathered, core_out, core_in,
    upper, lower, inverse, stacked,
    load_sem, send_sem, recv_sem, swap_send, swap_recv,
):
    grp = lax.axis_index("grp")
    slab = lax.axis_index("slab")
    core = lax.rem(slab, 2)
    chip = grp * 16 + slab // 2

    def peer(t):
        return (t // 16, lax.rem(t, 16) * 2 + core)

    twin = (grp, slab + 1 - 2 * core)

    def load(c):
        return pltpu.make_async_copy(
            tensor.at[pl.ds(c * CHUNK, CHUNK)], staged.at[c], load_sem.at[c]
        )

    for c in range(CHUNKS):
        load(c).start()

    barrier = pltpu.get_barrier_semaphore()

    def greet(k, carry):
        pl.semaphore_signal(
            barrier, inc=1, device_id=peer(lax.rem(chip + k, CHIPS)), device_id_type=MESH
        )
        return carry

    lax.fori_loop(1, CHIPS, greet, 0)
    pl.semaphore_signal(barrier, inc=1, device_id=twin, device_id_type=MESH)

    def set_block(x, rows):
        h, l = split(x)
        block[0:rows, :LANES] = h
        block[0:rows, LANES:] = l

    def pad_start(ref):
        width[...] = jnp.zeros_like(width)
        width[0:N, 0:RANK] = ref[...]
        set_block(width[...], NP)

    def prepare(c):
        load(c).wait()
        rows = pl.ds(c * CHUNK, CHUNK)
        h, l = split(staged[c, :, 0:640])
        high[rows, 0:640] = h
        low[rows, 0:640] = l
        h, l = split(staged[c, :, 640:N])
        high[rows, 640:N] = h
        low[rows, 640:N] = l

    def project(c):
        rows = pl.ds(c * CHUNK, CHUNK)
        v = block[...]
        return halves(dot(high[rows, :], v, NN) + dot(low[rows, :], v, NN))

    def product_one(first):
        total = None
        for c in range(CHUNKS):
            rows = pl.ds(c * CHUNK, CHUNK)
            if first:
                prepare(c)
            yh, yl = split(project(c))
            y = jnp.concatenate([yh, yl], axis=1)
            part = tops(dot(y, high[rows, :], NT) + dot(y, low[rows, :], NT))
            total = part if total is None else total + part
        width[...] = total.T

    def product_two():
        v = block[0:N, :]
        z = halves(dot(rhigh[...], v, NT) + dot(rlow[...], v, NT))
        zh, zl = split(z)
        zz = jnp.concatenate([zh, zl], axis=1)
        width[0:N, :] = halves(dot(rhigh[...], zz, NN) + dot(rlow[...], zz, NN))

    def pack(r):
        tail = width[3 * FOLD : N, :]
        keep = lane((FOLD, LANES)) < RANK
        tiles = FOLD // 8
        for b in range(3):
            body = width[b * FOLD : (b + 1) * FOLD, :]
            moved = pltpu.roll(tail, RANK - 32 * b, 1)
            packed[r, b * tiles : (b + 1) * tiles] = jnp.where(keep, body, moved).reshape(
                tiles, 8, LANES
            )
        packed[r, 63] = jnp.zeros((8, LANES), F32)

    def unpack(r):
        squares = gathered[r, 0] * gathered[r, 0]
        for t in range(1, CHIPS):
            squares = squares + gathered[r, t] * gathered[r, t]
        scale = lax.rsqrt(jnp.sum(jnp.sum(squares, axis=1, keepdims=True), axis=0, keepdims=True))
        lanes = lane((FOLD, LANES))
        tiles = FOLD // 8
        tail = jnp.zeros((FOLD, LANES), F32)
        for b in range(3):
            x = gathered[r, b * tiles : (b + 1) * tiles].reshape(FOLD, LANES) * scale
            h, l = split(jnp.where(lanes < RANK, x, 0.0))
            block[b * FOLD : (b + 1) * FOLD, :LANES] = h
            block[b * FOLD : (b + 1) * FOLD, LANES:] = l
            moved = pltpu.roll(x, 32 * b + 32, 1)
            tail = jnp.where((lanes >= 32 * b) & (lanes < 32 * b + 32), moved, tail)
        h, l = split(tail)
        block[3 * FOLD : N, :LANES] = h
        block[3 * FOLD : N, LANES:] = l

    def send_tiles(r, k, src, dst, stage):
        t = lax.rem(chip + k, CHIPS)
        return pltpu.make_async_remote_copy(
            src_ref=src.at[r, t if stage == 0 else chip],
            dst_ref=dst.at[r, chip],
            send_sem=send_sem.at[r, stage],
            recv_sem=recv_sem.at[r, stage],
            device_id=peer(t),
            device_id_type=MESH,
        )

    def send_all(r, src, dst, stage):
        def seven(i, carry):
            for u in range(7):
                send_tiles(r, 1 + 7 * i + u, src, dst, stage).start()
            return carry

        lax.fori_loop(0, 9, seven, 0)

    def bytes_of(ref, r, sem):
        part = ref.at[r, pl.ds(0, CHIPS - 1)]
        return pltpu.make_async_copy(part, part, sem)

    def reduce_block(r, first=None, last=None):
        pack(r)
        if r == 0:
            pl.semaphore_wait(barrier, CHIPS)
        send_all(r, packed, summed, 0)
        summed[r, pl.ds(chip, 1)] = packed[r, pl.ds(chip, 1)]
        if first is not None:
            first()
        bytes_of(summed, r, recv_sem.at[r, 0]).wait()
        total = summed[r, 0]
        for t in range(1, CHIPS):
            total = total + summed[r, t]
        pair[r, pl.ds(core, 1)] = total[None]
        twin_copy = pltpu.make_async_remote_copy(
            src_ref=pair.at[r, core],
            dst_ref=pair.at[r, core],
            send_sem=send_sem.at[r, 1],
            recv_sem=recv_sem.at[r, 1],
            device_id=twin,
            device_id_type=MESH,
        )
        twin_copy.start()
        twin_copy.wait()
        gathered[r, pl.ds(chip, 1)] = (pair[r, 0] + pair[r, 1])[None]
        send_all(r, gathered, gathered, 2)
        if last is not None:
            last()
        bytes_of(gathered, r, recv_sem.at[r, 2]).wait()
        bytes_of(packed, r, send_sem.at[r, 0]).wait()
        bytes_of(gathered, r, send_sem.at[r, 2]).wait()
        unpack(r)

    def cross_of():
        v = block[...]
        x = tops(halves(dot(v, v, NT)))
        upper[...] = x[0:RANK, :]
        rows = lax.broadcasted_iota(jnp.int32, (RANK, LANES), 0)
        lower[...] = jnp.where(rows == lane((RANK, LANES)), 1.0, 0.0)

    def panel(p, tiles):
        start = pl.multiple_of(8 * p, 8)
        u = upper[pl.ds(start, 8), :]
        w = lower[pl.ds(start, 8), :]
        sub = lax.broadcasted_iota(jnp.int32, (8, LANES), 0)
        full = (8, LANES)
        cols = [jnp.broadcast_to(u[:, j : j + 1], full) for j in range(8)]
        urow, wrow, inv, elem = [], [], [], {}
        pivots = jnp.ones(full, F32)
        for j in range(8):
            pivot = jnp.broadcast_to(cols[j][j : j + 1, :], full)
            inv.append(1.0 / pivot)
            pivots = jnp.where(sub == j, pivot, pivots)
            factor = jnp.where(sub > j, cols[j] * inv[j], 0.0)
            urow.append(jnp.broadcast_to(u[j : j + 1, :], full))
            wrow.append(jnp.broadcast_to(w[j : j + 1, :], full))
            u = u - factor * urow[j]
            w = w - factor * wrow[j]
            for k in range(j + 1, 8):
                elem[j, k] = jnp.broadcast_to(cols[k][j : j + 1, :], full)
                cols[k] = cols[k] - factor * elem[j, k]
        inverse[pl.ds(start, 8), :] = w * lax.rsqrt(pivots)
        for t in tiles:
            u = upper[8 * t : 8 * t + 8, :]
            w = lower[8 * t : 8 * t + 8, :]
            cols = [jnp.broadcast_to(u[:, j : j + 1], full) for j in range(8)]
            for j in range(8):
                factor = cols[j] * inv[j]
                u = u - factor * urow[j]
                w = w - factor * wrow[j]
                for k in range(j + 1, 8):
                    cols[k] = cols[k] - factor * elem[j, k]
            upper[8 * t : 8 * t + 8, :] = pltpu.roll(u, LANES - 8, 1)
            lower[8 * t : 8 * t + 8, :] = w

    def panels(first, last):
        def step(p, carry):
            panel(p, range(first + 1, 12))
            return carry

        lax.fori_loop(first, last, step, 0)

    def stack():
        h, l = split(inverse[...])
        stacked[:LANES, :] = h
        stacked[LANES:, :] = l

    def factor_start():
        cross_of()
        panels(0, 4)

    def factor_end():
        panels(4, 8)
        panels(8, 12)
        stack()

    def apply(rows):
        f = stacked[...]
        return halves(dot(block[rows, :LANES], f, TN) + dot(block[rows, LANES:], f, TN))

    high[:, 640:NP] = jnp.zeros((high.shape[0], LANES), BF16)
    low[:, 640:NP] = jnp.zeros((low.shape[0], LANES), BF16)
    inverse[...] = jnp.zeros_like(inverse)
    pad_start(start_one)
    product_one(True)
    reduce_block(0)
    product_one(False)
    reduce_block(1, factor_start, factor_end)
    set_block(apply(slice(0, NP)), NP)

    for c in range(CHUNKS):
        rtilde[c * CHUNK : (c + 1) * CHUNK, :] = project(c)
    for m in range(COLS):
        mode[m // 2, m % 2] = rtilde[pl.ds(m, ROWS, stride=COLS), :]

    def swap(src, dst, k, r):
        g = lax.rem(grp + k, GRP)
        return pltpu.make_async_remote_copy(
            src_ref=src.at[g],
            dst_ref=dst.at[grp],
            send_sem=swap_send.at[r],
            recv_sem=swap_recv.at[r],
            device_id=(g, slab),
            device_id_type=MESH,
        )

    for k in (2, 1, 3):
        swap(mode, given, k, 0).start()
    given[pl.ds(grp, 1)] = mode[pl.ds(grp, 1)]
    factor_start()
    factor_end()
    out_one[...] = apply(slice(0, N))[:, :RANK]
    part = given.at[pl.ds(0, GRP - 1)]
    pltpu.make_async_copy(part, part, swap_recv.at[0]).wait()
    part = mode.at[pl.ds(0, GRP - 1)]
    pltpu.make_async_copy(part, part, swap_send.at[0]).wait()
    f = stacked[...]
    for g in range(GRP):
        for m in range(2):
            h, l = split(given[g, m])
            h, l = split(halves(dot(h, f, TN) + dot(l, f, TN)))
            rhigh[g * ROWS : (g + 1) * ROWS, m * LANES : (m + 1) * LANES] = h
            rlow[g * ROWS : (g + 1) * ROWS, m * LANES : (m + 1) * LANES] = l

    pad_start(start_two)
    product_two()
    reduce_block(2)
    product_two()
    reduce_block(3, factor_start, factor_end)
    set_block(apply(slice(0, NP)), NP)
    v = block[0:N, :]
    partial = tops(dot(v, rhigh[...], NT) + dot(v, rlow[...], NT))
    factor_start()
    factor_end()
    out_two[...] = apply(slice(0, N))[:, :RANK]
    whole = jnp.dot(inverse[...], partial, precision=lax.Precision.HIGHEST)
    for g in range(GRP):
        for m in range(2):
            core_out[g, m] = whole[g * 24 : (g + 1) * 24, m * LANES : (m + 1) * LANES]
    for k in (2, 1, 3):
        swap(core_out, core_in, k, 1).start()
    core_in[pl.ds(grp, 1)] = core_out[pl.ds(grp, 1)]
    part = core_in.at[pl.ds(0, GRP - 1)]
    pltpu.make_async_copy(part, part, swap_recv.at[1]).wait()
    part = core_out.at[pl.ds(0, GRP - 1)]
    pltpu.make_async_copy(part, part, swap_send.at[1]).wait()
    for g in range(GRP):
        for m in range(2):
            out_core[pl.ds(2 * g + m, 24, stride=COLS), :] = core_in[g, m][:, :RANK]


def local(tensor, start_one, start_two):
    rows = ROWS * COLS
    vmem = pl.BlockSpec(memory_space=pltpu.VMEM)
    basis_one, basis_two, core = pl.pallas_call(
        kernel,
        out_shape=(
            jax.ShapeDtypeStruct((N, RANK), F32),
            jax.ShapeDtypeStruct((N, RANK), F32),
            jax.ShapeDtypeStruct((RANK // GRP * COLS, RANK), F32),
        ),
        in_specs=[pl.BlockSpec(memory_space=pl.ANY), vmem, vmem],
        out_specs=(vmem, vmem, vmem),
        scratch_shapes=[
            pltpu.VMEM((CHUNKS, CHUNK, N), F32),
            pltpu.VMEM((rows, NP), BF16),
            pltpu.VMEM((rows, NP), BF16),
            pltpu.VMEM((NP, 2 * LANES), BF16),
            pltpu.VMEM((NP, LANES), F32),
            pltpu.VMEM((N, 2 * LANES), BF16),
            pltpu.VMEM((N, 2 * LANES), BF16),
            pltpu.VMEM((rows, LANES), F32),
            pltpu.VMEM((GRP, 2, ROWS, LANES), F32),
            pltpu.VMEM((GRP, 2, ROWS, LANES), F32),
            pltpu.VMEM((4, CHIPS, 8, LANES), F32),
            pltpu.VMEM((4, CHIPS, 8, LANES), F32),
            pltpu.VMEM((4, 2, 8, LANES), F32),
            pltpu.VMEM((4, CHIPS, 8, LANES), F32),
            pltpu.VMEM((GRP, 2, 24, LANES), F32),
            pltpu.VMEM((GRP, 2, 24, LANES), F32),
            pltpu.VMEM((RANK, LANES), F32),
            pltpu.VMEM((RANK, LANES), F32),
            pltpu.VMEM((LANES, LANES), F32),
            pltpu.VMEM((2 * LANES, LANES), BF16),
            pltpu.SemaphoreType.DMA((CHUNKS,)),
            pltpu.SemaphoreType.DMA((4, 3)),
            pltpu.SemaphoreType.DMA((4, 3)),
            pltpu.SemaphoreType.DMA((2,)),
            pltpu.SemaphoreType.DMA((2,)),
        ],
        compiler_params=pltpu.CompilerParams(
            collective_id=0, has_side_effects=True, vmem_limit_bytes=48 << 20
        ),
    )(tensor.reshape(rows, N), start_one, start_two)
    return basis_one, basis_two, core.reshape(RANK // GRP, COLS, RANK)


def solution(mesh):
    in_specs = (P("grp", "slab", None), P(), P())
    out_specs = (P(), P(), P("grp", "slab", None))
    return jax.shard_map(local, mesh=mesh, in_specs=in_specs, out_specs=out_specs, check_vma=False)
```

```python
import jax
import jax.numpy as jnp
from jax import lax
from jax.experimental import pallas as pl
from jax.experimental.pallas import tpu as pltpu
from jax.sharding import PartitionSpec as P

MESH = pl.DeviceIdType.MESH
F32 = jnp.float32
BF16 = jnp.bfloat16

N = 672
NP = 768
RANK = 96
LANES = 128
GRP = 4
COLS = 8
ROWS = N // GRP
CHUNK = 448
CHUNKS = ROWS * COLS // CHUNK
CHIPS = 64
BODY, TAIL = 256, 80
FOLD = N // 4
OFFSETS = [(z, y, x) for z in range(4) for y in range(4) for x in range(4)]
FAR_FIRST = sorted(OFFSETS[1:], key=lambda o: -sum(min(d, 4 - d) for d in o))
NT = (((0,), (0,)), ((), ()))
NN = (((1,), (0,)), ((), ()))
TN = (((1,), (1,)), ((), ()))


def dot(a, b, dims):
    return lax.dot_general(a, b, dims, preferred_element_type=F32)


def split(x):
    high = x.astype(BF16)
    return high, (x - high.astype(F32)).astype(BF16)


def halves(x):
    return x[:, :LANES] + x[:, LANES:]


def tops(x):
    return x[:LANES] + x[LANES:]


def lane(shape):
    return lax.broadcasted_iota(jnp.int32, shape, len(shape) - 1)


def kernel(
    tensor, start_one, start_two, out_one, out_two, out_core,
    staged, starts, wide, gram, cross_part, ghigh, glow, high, low, block, exact, width, rhigh, rlow, rtilde, line, mode, given,
    packed, summed, pair, gathered, core_out, core_in,
    upper, lower, inverse, stacked,
    load_sem, send_sem, recv_sem, swap_send, swap_recv,
):
    grp = lax.axis_index("grp")
    slab = lax.axis_index("slab")
    core = lax.rem(slab, 2)
    chip = grp * 16 + slab // 2

    def peer(t):
        return (t // 16, lax.rem(t, 16) * 2 + core)

    zs = [grp] + [lax.rem(grp + d, 4) for d in range(1, 4)]
    ys = [lax.rem(slab // 8 + d, 4) * 4 for d in range(4)]
    xs = [lax.rem(slab // 2 + d, 4) for d in range(4)]
    twin = (grp, slab + 1 - 2 * core)

    def load(c):
        return pltpu.make_async_copy(
            tensor.at[pl.ds(c * CHUNK, CHUNK)], staged.at[c], load_sem.at[c]
        )

    def load_start(i):
        return pltpu.make_async_copy(
            (start_one, start_two)[i], starts.at[i], load_sem.at[CHUNKS + i]
        )

    load_start(0).start()
    for c in range(CHUNKS):
        load(c).start()
    load_start(1).start()

    barrier = pltpu.get_barrier_semaphore()

    def greet(k, carry):
        pl.semaphore_signal(
            barrier, inc=1, device_id=peer(lax.rem(chip + k, CHIPS)), device_id_type=MESH
        )
        return carry

    lax.fori_loop(1, CHIPS, greet, 0)
    pl.semaphore_signal(barrier, inc=1, device_id=twin, device_id_type=MESH)

    def set_block(x, rows):
        exact[0:rows, :] = x[0:rows]
        h, l = split(x)
        block[0:rows, :LANES] = h
        block[0:rows, LANES:] = l

    def pad_start(i):
        load_start(i).wait()
        wide[0:RANK, 0:N] = starts[i]
        set_block(wide[...].T, NP)

    def prepare(c):
        load(c).wait()
        rows = pl.ds(c * CHUNK, CHUNK)
        h, l = split(staged[c, :, 0:640])
        high[rows, 0:640] = h
        low[rows, 0:640] = l
        h, l = split(staged[c, :, 640:N])
        high[rows, 640:N] = h
        low[rows, 640:N] = l

    def project(c):
        rows = pl.ds(c * CHUNK, CHUNK)
        v = block[...]
        return halves(dot(high[rows, :], v, NN) + dot(low[rows, :], v, NN))

    def product_one():
        total = None
        for c in range(CHUNKS):
            rows = pl.ds(c * CHUNK, CHUNK)
            prepare(c)
            yh, yl = split(project(c))
            y = jnp.concatenate([yh, yl], axis=1)
            part = tops(dot(y, high[rows, :], NT) + dot(y, low[rows, :], NT))
            total = part if total is None else total + part
        width[...] = total.T

    def gram_high():
        for i in range(3):
            a = high[:, i * 256 : (i + 1) * 256]
            gram[i * 256 : (i + 1) * 256, i * 256 :] = dot(a, high[:, i * 256 :], NT)

    def gram_low():
        for i in range(3):
            a = high[:, i * 256 : (i + 1) * 256]
            cross_part[i * 256 : (i + 1) * 256, :] = dot(a, low[...], NT)
        for i in range(3):
            for j in range(i, 3):
                a, b = slice(i * 256, (i + 1) * 256), slice(j * 256, (j + 1) * 256)
                x = gram[a, b] + cross_part[a, b] + cross_part[b, a].T
                ghigh[a, b], glow[a, b] = split(x)
                if i != j:
                    ghigh[b, a], glow[b, a] = split(x.T)

    def product_gram():
        v = block[...]
        width[...] = halves(dot(ghigh[...], v, NN) + dot(glow[...], v, NN))

    def product_two():
        v = block[0:N, :]
        z = halves(dot(rhigh[...], v, NT) + dot(rlow[...], v, NT))
        zh, zl = split(z)
        zz = jnp.concatenate([zh, zl], axis=1)
        width[0:N, :] = halves(dot(rhigh[...], zz, NN) + dot(rlow[...], zz, NN))

    def pack(r):
        tail = width[3 * FOLD : N, :]
        keep = lane((FOLD, LANES)) < RANK
        tiles = FOLD // 8
        for b in range(3):
            body = width[b * FOLD : (b + 1) * FOLD, :]
            moved = pltpu.roll(tail, RANK - 32 * b, 1)
            packed[r, b * tiles : (b + 1) * tiles] = jnp.where(keep, body, moved).reshape(
                tiles, 8, LANES
            )
        packed[r, 63] = jnp.zeros((8, LANES), F32)

    def unpack(r):
        squares = gathered[r, 0] * gathered[r, 0]
        for t in range(1, CHIPS):
            squares = squares + gathered[r, t] * gathered[r, t]
        scale = lax.rsqrt(jnp.sum(jnp.sum(squares, axis=1, keepdims=True), axis=0, keepdims=True))
        lanes = lane((FOLD, LANES))
        tiles = FOLD // 8
        tail = jnp.zeros((FOLD, LANES), F32)
        for b in range(3):
            x = gathered[r, b * tiles : (b + 1) * tiles].reshape(FOLD, LANES) * scale
            x0 = jnp.where(lanes < RANK, x, 0.0)
            exact[b * FOLD : (b + 1) * FOLD, :] = x0
            h, l = split(x0)
            block[b * FOLD : (b + 1) * FOLD, :LANES] = h
            block[b * FOLD : (b + 1) * FOLD, LANES:] = l
            moved = pltpu.roll(x, 32 * b + 32, 1)
            tail = jnp.where((lanes >= 32 * b) & (lanes < 32 * b + 32), moved, tail)
        exact[3 * FOLD : N, :] = tail
        h, l = split(tail)
        block[3 * FOLD : N, :LANES] = h
        block[3 * FOLD : N, LANES:] = l

    def send_all(r, src, dst, stage):
        for dz, dy, dx in FAR_FIRST:
            part = ys[dy] + xs[dx]
            pltpu.make_async_remote_copy(
                src_ref=src.at[r, zs[dz] * 16 + part if stage == 0 else chip],
                dst_ref=dst.at[r, chip],
                send_sem=send_sem.at[r, stage],
                recv_sem=recv_sem.at[r, stage],
                device_id=(zs[dz], part * 2 + core),
                device_id_type=MESH,
            ).start()

    def bytes_of(ref, r, sem):
        part = ref.at[r, pl.ds(0, CHIPS - 1)]
        return pltpu.make_async_copy(part, part, sem)

    def reduce_block(r, first=None, last=None):
        pack(r)
        if r == 0:
            pl.semaphore_wait(barrier, CHIPS)
        send_all(r, packed, summed, 0)
        summed[r, pl.ds(chip, 1)] = packed[r, pl.ds(chip, 1)]
        if first is not None:
            first()
        bytes_of(summed, r, recv_sem.at[r, 0]).wait()
        total = summed[r, 0]
        for t in range(1, CHIPS):
            total = total + summed[r, t]
        pair[r, pl.ds(core, 1)] = total[None]
        twin_copy = pltpu.make_async_remote_copy(
            src_ref=pair.at[r, core],
            dst_ref=pair.at[r, core],
            send_sem=send_sem.at[r, 1],
            recv_sem=recv_sem.at[r, 1],
            device_id=twin,
            device_id_type=MESH,
        )
        twin_copy.start()
        twin_copy.wait()
        gathered[r, pl.ds(chip, 1)] = (pair[r, 0] + pair[r, 1])[None]
        send_all(r, gathered, gathered, 2)
        if last is not None:
            last()
        bytes_of(gathered, r, recv_sem.at[r, 2]).wait()
        bytes_of(packed, r, send_sem.at[r, 0]).wait()
        bytes_of(gathered, r, send_sem.at[r, 2]).wait()
        unpack(r)

    def cross_of():
        v = exact[0:N, :]
        x = lax.dot_general(v, v, NT, precision=lax.Precision.HIGHEST, preferred_element_type=F32)
        upper[...] = x[0:RANK, :]
        rows = lax.broadcasted_iota(jnp.int32, (RANK, LANES), 0)
        lower[...] = jnp.where(rows == lane((RANK, LANES)), 1.0, 0.0)

    def panel(p, tiles):
        start = pl.multiple_of(8 * p, 8)
        u = upper[pl.ds(start, 8), :]
        w = lower[pl.ds(start, 8), :]
        sub = lax.broadcasted_iota(jnp.int32, (8, LANES), 0)
        full = (8, LANES)
        cols = [jnp.broadcast_to(u[:, j : j + 1], full) for j in range(8)]
        urow, wrow, inv, elem = [], [], [], {}
        pivots = jnp.ones(full, F32)
        for j in range(8):
            pivot = jnp.broadcast_to(cols[j][j : j + 1, :], full)
            inv.append(1.0 / pivot)
            pivots = jnp.where(sub == j, pivot, pivots)
            factor = jnp.where(sub > j, cols[j] * inv[j], 0.0)
            urow.append(jnp.broadcast_to(u[j : j + 1, :], full))
            wrow.append(jnp.broadcast_to(w[j : j + 1, :], full))
            u = u - factor * urow[j]
            w = w - factor * wrow[j]
            for k in range(j + 1, 8):
                elem[j, k] = jnp.broadcast_to(cols[k][j : j + 1, :], full)
                cols[k] = cols[k] - factor * elem[j, k]
        inverse[pl.ds(start, 8), :] = w * lax.rsqrt(pivots)
        for t in tiles:
            u = upper[8 * t : 8 * t + 8, :]
            w = lower[8 * t : 8 * t + 8, :]
            cols = [jnp.broadcast_to(u[:, j : j + 1], full) for j in range(8)]
            for j in range(8):
                factor = cols[j] * inv[j]
                u = u - factor * urow[j]
                w = w - factor * wrow[j]
                for k in range(j + 1, 8):
                    cols[k] = cols[k] - factor * elem[j, k]
            upper[8 * t : 8 * t + 8, :] = pltpu.roll(u, LANES - 8, 1)
            lower[8 * t : 8 * t + 8, :] = w

    def panels(first, last):
        def step(p, carry):
            panel(p, range(first + 1, 12))
            return carry

        lax.fori_loop(first, last, step, 0)

    def stack():
        h, l = split(inverse[...])
        stacked[:LANES, :] = h
        stacked[LANES:, :] = l

    def factor_start():
        cross_of()
        panels(0, 4)

    def factor_end():
        panels(4, 8)
        panels(8, 12)
        stack()

    def basis():
        return lax.dot_general(
            inverse[0:RANK, :], exact[0:N, :], TN,
            precision=lax.Precision.HIGHEST, preferred_element_type=F32,
        )

    def apply(rows):
        return lax.dot_general(exact[rows, :], inverse[...], TN, precision=lax.Precision.HIGHEST, preferred_element_type=F32)

    high[:, 640:NP] = jnp.zeros((high.shape[0], LANES), BF16)
    low[:, 640:NP] = jnp.zeros((low.shape[0], LANES), BF16)
    inverse[...] = jnp.zeros_like(inverse)
    wide[...] = jnp.zeros_like(wide)
    pad_start(0)
    product_one()
    reduce_block(0, gram_high, gram_low)
    product_gram()
    reduce_block(1, factor_start, factor_end)
    set_block(apply(slice(0, NP)), NP)

    for c in range(CHUNKS):
        rtilde[c * CHUNK : (c + 1) * CHUNK, :] = project(c)
    keep = lane((TAIL, LANES)) < RANK
    for g in range(GRP):
        line[0:ROWS, :] = rtilde[pl.ds(2 * g, ROWS, stride=COLS), :]
        line[ROWS:, :] = rtilde[pl.ds(2 * g + 1, ROWS, stride=COLS), :]
        tail = line[BODY:, :]
        for b in range(3):
            rows = slice(b * TAIL, (b + 1) * TAIL)
            mode[g, rows] = jnp.where(keep, line[rows, :], pltpu.roll(tail, RANK - 32 * b, 1))
        mode[g, 3 * TAIL : BODY] = line[3 * TAIL : BODY, :]

    def swap(src, dst, k, r):
        g = lax.rem(grp + k, GRP)
        return pltpu.make_async_remote_copy(
            src_ref=src.at[g],
            dst_ref=dst.at[grp],
            send_sem=swap_send.at[r],
            recv_sem=swap_recv.at[r],
            device_id=(g, slab),
            device_id_type=MESH,
        )

    for k in (2, 1, 3):
        swap(mode, given, k, 0).start()
    given[pl.ds(grp, 1)] = mode[pl.ds(grp, 1)]
    factor_start()
    factor_end()
    out_one[...] = basis()
    part = given.at[pl.ds(0, GRP - 1)]
    pltpu.make_async_copy(part, part, swap_recv.at[0]).wait()
    part = mode.at[pl.ds(0, GRP - 1)]
    pltpu.make_async_copy(part, part, swap_send.at[0]).wait()
    f = stacked[...]
    lanes = lane((TAIL, LANES))
    for g in range(GRP):
        tail = jnp.zeros((TAIL, LANES), F32)
        for b in range(3):
            x = given[g, b * TAIL : (b + 1) * TAIL]
            line[b * TAIL : (b + 1) * TAIL, :] = jnp.where(lanes < RANK, x, 0.0)
            inside = (lanes >= 32 * b) & (lanes < 32 * b + 32)
            tail = jnp.where(inside, pltpu.roll(x, 32 * b + 32, 1), tail)
        line[3 * TAIL : BODY, :] = given[g, 3 * TAIL : BODY]
        line[BODY:, :] = tail
        h, l = split(line[...])
        y = halves(dot(h, f, TN) + dot(l, f, TN))
        for m in range(2):
            h, l = split(y[m * ROWS : (m + 1) * ROWS])
            rhigh[g * ROWS : (g + 1) * ROWS, m * LANES : (m + 1) * LANES] = h
            rlow[g * ROWS : (g + 1) * ROWS, m * LANES : (m + 1) * LANES] = l

    width[N:NP, :] = jnp.zeros((NP - N, LANES), F32)
    pad_start(1)
    product_two()
    reduce_block(2)
    product_two()
    reduce_block(3, factor_start, factor_end)
    set_block(apply(slice(0, NP)), NP)
    v = block[0:N, :]
    partial = tops(dot(v, rhigh[...], NT) + dot(v, rlow[...], NT))
    factor_start()
    factor_end()
    out_two[...] = basis()
    whole = jnp.dot(inverse[...], partial, precision=lax.Precision.HIGHEST)
    for g in range(GRP):
        for m in range(2):
            core_out[g, m] = whole[g * 24 : (g + 1) * 24, m * LANES : (m + 1) * LANES]
    for k in (2, 1, 3):
        swap(core_out, core_in, k, 1).start()
    core_in[pl.ds(grp, 1)] = core_out[pl.ds(grp, 1)]
    part = core_in.at[pl.ds(0, GRP - 1)]
    pltpu.make_async_copy(part, part, swap_recv.at[1]).wait()
    part = core_out.at[pl.ds(0, GRP - 1)]
    pltpu.make_async_copy(part, part, swap_send.at[1]).wait()
    for g in range(GRP):
        for m in range(2):
            out_core[pl.ds(2 * g + m, 24, stride=COLS), :] = core_in[g, m][:, :RANK]


def local(tensor, start_one, start_two):
    rows = ROWS * COLS
    vmem = pl.BlockSpec(memory_space=pltpu.VMEM)
    hbm = pl.BlockSpec(memory_space=pltpu.HBM)
    basis_one, basis_two, core = pl.pallas_call(
        kernel,
        out_shape=(
            jax.ShapeDtypeStruct((RANK, N), F32),
            jax.ShapeDtypeStruct((RANK, N), F32),
            jax.ShapeDtypeStruct((RANK // GRP * COLS, RANK), F32),
        ),
        in_specs=[hbm, hbm, hbm],
        out_specs=(vmem, vmem, vmem),
        scratch_shapes=[
            pltpu.VMEM((CHUNKS, CHUNK, N), F32),
            pltpu.VMEM((2, RANK, N), F32),
            pltpu.VMEM((LANES, NP), F32),
            pltpu.VMEM((NP, NP), F32),
            pltpu.VMEM((NP, NP), F32),
            pltpu.VMEM((NP, NP), BF16),
            pltpu.VMEM((NP, NP), BF16),
            pltpu.VMEM((rows, NP), BF16),
            pltpu.VMEM((rows, NP), BF16),
            pltpu.VMEM((NP, 2 * LANES), BF16),
            pltpu.VMEM((NP, LANES), F32),
            pltpu.VMEM((NP, LANES), F32),
            pltpu.VMEM((N, 2 * LANES), BF16),
            pltpu.VMEM((N, 2 * LANES), BF16),
            pltpu.VMEM((rows, LANES), F32),
            pltpu.VMEM((2 * ROWS, LANES), F32),
            pltpu.VMEM((GRP, BODY, LANES), F32),
            pltpu.VMEM((GRP, BODY, LANES), F32),
            pltpu.VMEM((4, CHIPS, 8, LANES), F32),
            pltpu.VMEM((4, CHIPS, 8, LANES), F32),
            pltpu.VMEM((4, 2, 8, LANES), F32),
            pltpu.VMEM((4, CHIPS, 8, LANES), F32),
            pltpu.VMEM((GRP, 2, 24, LANES), F32),
            pltpu.VMEM((GRP, 2, 24, LANES), F32),
            pltpu.VMEM((RANK, LANES), F32),
            pltpu.VMEM((RANK, LANES), F32),
            pltpu.VMEM((LANES, LANES), F32),
            pltpu.VMEM((2 * LANES, LANES), BF16),
            pltpu.SemaphoreType.DMA((CHUNKS + 2,)),
            pltpu.SemaphoreType.DMA((4, 3)),
            pltpu.SemaphoreType.DMA((4, 3)),
            pltpu.SemaphoreType.DMA((2,)),
            pltpu.SemaphoreType.DMA((2,)),
        ],
        compiler_params=pltpu.CompilerParams(
            collective_id=0, has_side_effects=True, vmem_limit_bytes=48 << 20
        ),
    )(
        pltpu.with_memory_space_constraint(tensor.reshape(rows, N), pltpu.HBM),
        pltpu.with_memory_space_constraint(start_one.T, pltpu.HBM),
        pltpu.with_memory_space_constraint(start_two.T, pltpu.HBM),
    )
    return basis_one.T, basis_two.T, core.reshape(RANK // GRP, COLS, RANK)


def solution(mesh):
    in_specs = (P("grp", "slab", None), P(), P())
    out_specs = (P(), P(), P("grp", "slab", None))
    return jax.shard_map(local, mesh=mesh, in_specs=in_specs, out_specs=out_specs, check_vma=False)
```

```python
import jax
import jax.numpy as jnp
from jax import lax
from jax.experimental import pallas as pl
from jax.experimental.pallas import tpu as pltpu
from jax.sharding import PartitionSpec as P

MESH = pl.DeviceIdType.MESH
F32 = jnp.float32
BF16 = jnp.bfloat16

N = 672
NP = 768
RANK = 96
LANES = 128
GRP = 4
COLS = 8
ROWS = N // GRP
CHUNK = 448
CHUNKS = ROWS * COLS // CHUNK
CHIPS = 64
STEP = CHUNK // COLS
BODY, TAIL = 88, 24
CORE_BODY, CORE_TAIL = 144, 48
FOLD = N // 4
OFFSETS = [(z, y, x) for z in range(4) for y in range(4) for x in range(4)]
FAR_FIRST = sorted(OFFSETS[1:], key=lambda o: -sum(min(d, 4 - d) for d in o))
NT = (((0,), (0,)), ((), ()))
NN = (((1,), (0,)), ((), ()))
TN = (((1,), (1,)), ((), ()))


def dot(a, b, dims):
    return lax.dot_general(a, b, dims, preferred_element_type=F32)


def split(x):
    high = x.astype(BF16)
    return high, (x - high.astype(F32)).astype(BF16)


def halves(x):
    return x[:, :LANES] + x[:, LANES:]


def tops(x):
    return x[:LANES] + x[LANES:]


def lane(shape):
    return lax.broadcasted_iota(jnp.int32, shape, len(shape) - 1)


def kernel(
    tensor, start_one, start_two, out_one, out_two, out_core,
    staged, starts, wide, gram, cross_part, ghigh, glow, high, low, block, exact, width, rhigh, rlow, rtilde, line, mode, given,
    packed, summed, pair, gathered, core_out, core_in,
    unit, upper, lower, inverse, stacked,
    load_sem, send_sem, recv_sem, swap_send, swap_recv,
):
    grp = lax.axis_index("grp")
    slab = lax.axis_index("slab")
    core = lax.rem(slab, 2)
    chip = grp * 16 + slab // 2

    def peer(t):
        return (t // 16, lax.rem(t, 16) * 2 + core)

    zs = [grp] + [lax.rem(grp + d, 4) for d in range(1, 4)]
    ys = [lax.rem(slab // 8 + d, 4) * 4 for d in range(4)]
    xs = [lax.rem(slab // 2 + d, 4) for d in range(4)]
    twin = (grp, slab + 1 - 2 * core)

    def load(c):
        return pltpu.make_async_copy(
            tensor.at[pl.ds(c * CHUNK, CHUNK)], staged.at[c], load_sem.at[c]
        )

    def load_start(i):
        return pltpu.make_async_copy(
            (start_one, start_two)[i], starts.at[i], load_sem.at[CHUNKS + i]
        )

    barrier = pltpu.get_barrier_semaphore()

    def greet(k, carry):
        pl.semaphore_signal(
            barrier, inc=1, device_id=peer(lax.rem(chip + k, CHIPS)), device_id_type=MESH
        )
        return carry

    lax.fori_loop(1, CHIPS, greet, 0)
    pl.semaphore_signal(barrier, inc=1, device_id=twin, device_id_type=MESH)

    load_start(0).start()
    for c in range(CHUNKS):
        load(c).start()
    load_start(1).start()

    def set_block(x, rows):
        exact[0:rows, :] = x[0:rows]
        h, l = split(x)
        block[0:rows, :LANES] = h
        block[0:rows, LANES:] = l

    def pad_start(i):
        load_start(i).wait()
        wide[0:RANK, 0:N] = starts[i]
        set_block(wide[...].T, NP)

    def prepare(c):
        load(c).wait()
        rows = pl.ds(c * CHUNK, CHUNK)
        x = staged[c, :, 0:640]
        squares = jnp.sum((x * x).reshape(CHUNK // 8, 8, 640), axis=0)
        for k in range(5):
            packed[0, 63] += squares[:, k * LANES : (k + 1) * LANES]
        h, l = split(x)
        high[rows, 0:640] = h
        low[rows, 0:640] = l
        x = staged[c, :, 640:N]
        packed[0, 63, :, 0 : N - 640] += jnp.sum((x * x).reshape(CHUNK // 8, 8, N - 640), axis=0)
        h, l = split(x)
        high[rows, 640:N] = h
        low[rows, 640:N] = l

    def project(c):
        rows = pl.ds(c * CHUNK, CHUNK)
        v = block[...]
        return halves(dot(high[rows, :], v, NN) + dot(low[rows, :], v, NN))

    def product_one():
        total = None
        for c in range(CHUNKS):
            rows = pl.ds(c * CHUNK, CHUNK)
            prepare(c)
            yh, yl = split(project(c))
            y = jnp.concatenate([yh, yl], axis=1)
            part = tops(dot(y, high[rows, :], NT) + dot(y, low[rows, :], NT))
            total = part if total is None else total + part
        width[...] = total.T

    def gram_high():
        for i in range(3):
            a = high[:, i * 256 : (i + 1) * 256]
            gram[i * 256 : (i + 1) * 256, i * 256 :] = dot(a, high[:, i * 256 :], NT)

    def gram_low():
        for i in range(3):
            a = high[:, i * 256 : (i + 1) * 256]
            cross_part[i * 256 : (i + 1) * 256, :] = dot(a, low[...], NT)
        for i in range(3):
            for j in range(i, 3):
                a, b = slice(i * 256, (i + 1) * 256), slice(j * 256, (j + 1) * 256)
                x = gram[a, b] + cross_part[a, b] + cross_part[b, a].T
                ghigh[a, b], glow[a, b] = split(x)
                if i != j:
                    ghigh[b, a], glow[b, a] = split(x.T)

    def product_gram():
        v = block[...]
        width[...] = halves(dot(ghigh[...], v, NN) + dot(glow[...], v, NN))

    def product_two():
        v = block[0:N, :]
        z = halves(dot(rhigh[...], v, NT) + dot(rlow[...], v, NT))
        zh, zl = split(z)
        zz = jnp.concatenate([zh, zl], axis=1)
        width[0:N, :] = halves(dot(rhigh[...], zz, NN) + dot(rlow[...], zz, NN))

    def pack(r):
        tail = width[3 * FOLD : N, :]
        keep = lane((FOLD, LANES)) < RANK
        tiles = FOLD // 8
        for b in range(3):
            body = width[b * FOLD : (b + 1) * FOLD, :]
            moved = pltpu.roll(tail, RANK - 32 * b, 1)
            packed[r, b * tiles : (b + 1) * tiles] = jnp.where(keep, body, moved).reshape(
                tiles, 8, LANES
            )

    def unpack(r):
        if r == 0:
            squares = gathered[0, 63]
            trace = jnp.sum(jnp.sum(squares, axis=1, keepdims=True), axis=0, keepdims=True)
            unit[...] = jnp.broadcast_to(1.0 / trace, (8, LANES))
        scale = unit[0:1, :]
        lanes = lane((FOLD, LANES))
        tiles = FOLD // 8
        tail = jnp.zeros((FOLD, LANES), F32)
        for b in range(3):
            x = gathered[r, b * tiles : (b + 1) * tiles].reshape(FOLD, LANES) * scale
            x0 = jnp.where(lanes < RANK, x, 0.0)
            exact[b * FOLD : (b + 1) * FOLD, :] = x0
            h, l = split(x0)
            block[b * FOLD : (b + 1) * FOLD, :LANES] = h
            block[b * FOLD : (b + 1) * FOLD, LANES:] = l
            moved = pltpu.roll(x, 32 * b + 32, 1)
            tail = jnp.where((lanes >= 32 * b) & (lanes < 32 * b + 32), moved, tail)
        exact[3 * FOLD : N, :] = tail
        h, l = split(tail)
        block[3 * FOLD : N, :LANES] = h
        block[3 * FOLD : N, LANES:] = l

    def send_all(r, src, dst, stage):
        for dz, dy, dx in FAR_FIRST:
            part = ys[dy] + xs[dx]
            pltpu.make_async_remote_copy(
                src_ref=src.at[r, zs[dz] * 16 + part if stage == 0 else chip],
                dst_ref=dst.at[r, chip],
                send_sem=send_sem.at[r, stage],
                recv_sem=recv_sem.at[r, stage],
                device_id=(zs[dz], part * 2 + core),
                device_id_type=MESH,
            ).start()

    def bytes_of(ref, r, sem):
        part = ref.at[r, pl.ds(0, CHIPS - 1)]
        return pltpu.make_async_copy(part, part, sem)

    def reduce_block(r, first=None, last=None):
        pack(r)
        if r == 0:
            pl.semaphore_wait(barrier, CHIPS)
        send_all(r, packed, summed, 0)
        summed[r, pl.ds(chip, 1)] = packed[r, pl.ds(chip, 1)]
        if first is not None:
            first()
        bytes_of(summed, r, recv_sem.at[r, 0]).wait()
        total = summed[r, 0]
        for t in range(1, CHIPS):
            total = total + summed[r, t]
        pair[r, pl.ds(core, 1)] = total[None]
        twin_copy = pltpu.make_async_remote_copy(
            src_ref=pair.at[r, core],
            dst_ref=pair.at[r, core],
            send_sem=send_sem.at[r, 1],
            recv_sem=recv_sem.at[r, 1],
            device_id=twin,
            device_id_type=MESH,
        )
        twin_copy.start()
        twin_copy.wait()
        gathered[r, pl.ds(chip, 1)] = (pair[r, 0] + pair[r, 1])[None]
        send_all(r, gathered, gathered, 2)
        if last is not None:
            last()
        bytes_of(gathered, r, recv_sem.at[r, 2]).wait()
        bytes_of(packed, r, send_sem.at[r, 0]).wait()
        bytes_of(gathered, r, send_sem.at[r, 2]).wait()
        unpack(r)

    def cross_of():
        v = exact[0:N, :]
        x = lax.dot_general(v, v, NT, precision=lax.Precision.HIGHEST, preferred_element_type=F32)
        upper[...] = x[0:RANK, :]
        rows = lax.broadcasted_iota(jnp.int32, (RANK, LANES), 0)
        lower[...] = jnp.where(rows == lane((RANK, LANES)), 1.0, 0.0)

    def panel(p, tiles):
        start = pl.multiple_of(8 * p, 8)
        u = upper[pl.ds(start, 8), :]
        w = lower[pl.ds(start, 8), :]
        sub = lax.broadcasted_iota(jnp.int32, (8, LANES), 0)
        full = (8, LANES)
        cols = [jnp.broadcast_to(u[:, j : j + 1], full) for j in range(8)]
        urow, wrow, inv, elem = [], [], [], {}
        pivots = jnp.ones(full, F32)
        for j in range(8):
            pivot = jnp.broadcast_to(cols[j][j : j + 1, :], full)
            inv.append(1.0 / pivot)
            pivots = jnp.where(sub == j, pivot, pivots)
            factor = jnp.where(sub > j, cols[j] * inv[j], 0.0)
            urow.append(jnp.broadcast_to(u[j : j + 1, :], full))
            wrow.append(jnp.broadcast_to(w[j : j + 1, :], full))
            u = u - factor * urow[j]
            w = w - factor * wrow[j]
            for k in range(j + 1, 8):
                elem[j, k] = jnp.broadcast_to(cols[k][j : j + 1, :], full)
                cols[k] = cols[k] - factor * elem[j, k]
        inverse[pl.ds(start, 8), :] = w * lax.rsqrt(pivots)
        for t in tiles:
            u = upper[8 * t : 8 * t + 8, :]
            w = lower[8 * t : 8 * t + 8, :]
            cols = [jnp.broadcast_to(u[:, j : j + 1], full) for j in range(8)]
            for j in range(8):
                factor = cols[j] * inv[j]
                u = u - factor * urow[j]
                w = w - factor * wrow[j]
                for k in range(j + 1, 8):
                    cols[k] = cols[k] - factor * elem[j, k]
            upper[8 * t : 8 * t + 8, :] = pltpu.roll(u, LANES - 8, 1)
            lower[8 * t : 8 * t + 8, :] = w

    def panels(first, last):
        def step(p, carry):
            panel(p, range(first + 1, 12))
            return carry

        lax.fori_loop(first, last, step, 0)

    def stack():
        h, l = split(inverse[...])
        stacked[:LANES, :] = h
        stacked[LANES:, :] = l

    def factor_start():
        cross_of()
        panels(0, 4)

    def factor_end():
        panels(4, 8)
        panels(8, 12)
        stack()

    def basis():
        return lax.dot_general(
            inverse[0:RANK, :], exact[0:N, :], TN,
            precision=lax.Precision.HIGHEST, preferred_element_type=F32,
        )

    def apply(rows):
        return lax.dot_general(exact[rows, :], inverse[...], TN, precision=lax.Precision.HIGHEST, preferred_element_type=F32)

    packed[:, 63] = jnp.zeros((4, 8, LANES), F32)
    high[:, 640:NP] = jnp.zeros((high.shape[0], LANES), BF16)
    low[:, 640:NP] = jnp.zeros((low.shape[0], LANES), BF16)
    inverse[...] = jnp.zeros_like(inverse)
    wide[...] = jnp.zeros_like(wide)
    pad_start(0)
    product_one()
    reduce_block(0, gram_high, gram_low)
    product_gram()
    reduce_block(1, factor_start, factor_end)
    set_block(apply(slice(0, N)), N)

    def fold(target, body, tail):
        keep = lane((tail, LANES)) < RANK
        end = line[body : body + tail, :]
        for b in range(3):
            rows = slice(b * tail, (b + 1) * tail)
            target[rows] = jnp.where(keep, line[rows, :], pltpu.roll(end, RANK - 32 * b, 1))
        if body > 3 * tail:
            target[3 * tail : body] = line[3 * tail : body, :]

    def unfold(source, start, body, tail):
        lanes = lane((tail, LANES))
        end = jnp.zeros((tail, LANES), F32)
        for b in range(3):
            x = source[b * tail : (b + 1) * tail]
            line[start + b * tail : start + (b + 1) * tail, :] = jnp.where(lanes < RANK, x, 0.0)
            inside = (lanes >= 32 * b) & (lanes < 32 * b + 32)
            end = jnp.where(inside, pltpu.roll(x, 32 * b + 32, 1), end)
        if body > 3 * tail:
            line[start + 3 * tail : start + body, :] = source[3 * tail : body]
        line[start + body : start + body + tail, :] = end

    def swap(src, dst, k, r):
        g = lax.rem(grp + k, GRP)
        return pltpu.make_async_remote_copy(
            src_ref=src(g),
            dst_ref=dst,
            send_sem=swap_send.at[r],
            recv_sem=swap_recv.at[r],
            device_id=(g, slab),
            device_id_type=MESH,
        )

    def three(ref, sem):
        part = ref.at[pl.ds(0, GRP - 1)]
        return pltpu.make_async_copy(part, part, sem)

    for c in range(CHUNKS):
        rtilde[c * CHUNK : (c + 1) * CHUNK, :] = project(c)
        for g in range(GRP):
            for m in range(2):
                line[m * STEP : (m + 1) * STEP, :] = rtilde[
                    pl.ds(c * CHUNK + 2 * g + m, STEP, stride=COLS), :
                ]
            fold(mode.at[c, g], BODY, TAIL)
        for k in (2, 1, 3):
            swap(lambda g: mode.at[c, g], given.at[c, grp], k, c).start()
        given[c, pl.ds(grp, 1)] = mode[c, pl.ds(grp, 1)]
    factor_start()
    factor_end()
    out_one[...] = basis()
    width[N:NP, :] = jnp.zeros((NP - N, LANES), F32)
    pad_start(1)
    f = stacked[...]
    for c in range(CHUNKS):
        three(given.at[c], swap_recv.at[c]).wait()
        size = 2 * STEP
        for g in range(GRP):
            unfold(given.at[c, g], g * size, BODY, TAIL)
        h, l = split(line[...])
        y = halves(dot(h, f, TN) + dot(l, f, TN))
        for g in range(GRP):
            rows = slice(g * ROWS + c * STEP, g * ROWS + (c + 1) * STEP)
            for m in range(2):
                h, l = split(y[g * size + m * STEP : g * size + (m + 1) * STEP])
                rhigh[rows, m * LANES : (m + 1) * LANES] = h
                rlow[rows, m * LANES : (m + 1) * LANES] = l
    for c in range(CHUNKS):
        three(mode.at[c], swap_send.at[c]).wait()

    product_two()
    reduce_block(2)
    product_two()
    reduce_block(3, factor_start, factor_end)
    set_block(apply(slice(0, N)), N)
    v = block[0:N, :]
    partial = tops(dot(v, rhigh[...], NT) + dot(v, rlow[...], NT))
    for m in range(2):
        line[m * RANK : (m + 1) * RANK, :] = partial[0:RANK, m * LANES : (m + 1) * LANES]
    fold(core_out, CORE_BODY, CORE_TAIL)
    for k in (2, 1, 3):
        swap(lambda g: core_out, core_in.at[grp], k, CHUNKS).start()
    core_in[pl.ds(grp, 1)] = core_out[...][None]
    factor_start()
    factor_end()
    out_two[...] = basis()
    mine = inverse[pl.ds(pl.multiple_of(grp * 24, 8), 24), 0:RANK]
    three(core_in, swap_recv.at[CHUNKS]).wait()
    for g in range(GRP):
        unfold(core_in.at[g], 0, CORE_BODY, CORE_TAIL)
        for m in range(2):
            x = line[m * RANK : (m + 1) * RANK, :]
            out_core[pl.ds(2 * g + m, 24, stride=COLS), :] = jnp.dot(
                mine, x, precision=lax.Precision.HIGHEST
            )[:, :RANK]
    for k in range(1, GRP):
        pltpu.make_async_copy(core_out, core_out, swap_send.at[CHUNKS]).wait()


def finish(one, two, core, out_one, out_two, out_core, sems):
    pairs = ((one, out_one), (two, out_two), (core, out_core))
    copies = [pltpu.make_async_copy(a, b, sems.at[i]) for i, (a, b) in enumerate(pairs)]
    for copy in copies:
        copy.start()
    for copy in copies:
        copy.wait()


def local(tensor, start_one, start_two):
    rows = ROWS * COLS
    vmem = pl.BlockSpec(memory_space=pltpu.VMEM)
    hbm = pl.BlockSpec(memory_space=pltpu.HBM)
    basis_one, basis_two, core = pl.pallas_call(
        kernel,
        out_shape=(
            jax.ShapeDtypeStruct((RANK, N), F32),
            jax.ShapeDtypeStruct((RANK, N), F32),
            jax.ShapeDtypeStruct((RANK // GRP * COLS, RANK), F32),
        ),
        in_specs=[hbm, hbm, hbm],
        out_specs=(vmem, vmem, vmem),
        scratch_shapes=[
            pltpu.VMEM((CHUNKS, CHUNK, N), F32),
            pltpu.VMEM((2, RANK, N), F32),
            pltpu.VMEM((LANES, NP), F32),
            pltpu.VMEM((NP, NP), F32),
            pltpu.VMEM((NP, NP), F32),
            pltpu.VMEM((NP, NP), BF16),
            pltpu.VMEM((NP, NP), BF16),
            pltpu.VMEM((rows, NP), BF16),
            pltpu.VMEM((rows, NP), BF16),
            pltpu.VMEM((NP, 2 * LANES), BF16),
            pltpu.VMEM((NP, LANES), F32),
            pltpu.VMEM((NP, LANES), F32),
            pltpu.VMEM((N, 2 * LANES), BF16),
            pltpu.VMEM((N, 2 * LANES), BF16),
            pltpu.VMEM((rows, LANES), F32),
            pltpu.VMEM((CHUNK, LANES), F32),
            pltpu.VMEM((CHUNKS, GRP, BODY, LANES), F32),
            pltpu.VMEM((CHUNKS, GRP, BODY, LANES), F32),
            pltpu.VMEM((4, CHIPS, 8, LANES), F32),
            pltpu.VMEM((4, CHIPS, 8, LANES), F32),
            pltpu.VMEM((4, 2, 8, LANES), F32),
            pltpu.VMEM((4, CHIPS, 8, LANES), F32),
            pltpu.VMEM((CORE_BODY, LANES), F32),
            pltpu.VMEM((GRP, CORE_BODY, LANES), F32),
            pltpu.VMEM((8, LANES), F32),
            pltpu.VMEM((RANK, LANES), F32),
            pltpu.VMEM((RANK, LANES), F32),
            pltpu.VMEM((LANES, LANES), F32),
            pltpu.VMEM((2 * LANES, LANES), BF16),
            pltpu.SemaphoreType.DMA((CHUNKS + 2,)),
            pltpu.SemaphoreType.DMA((4, 3)),
            pltpu.SemaphoreType.DMA((4, 3)),
            pltpu.SemaphoreType.DMA((CHUNKS + 1,)),
            pltpu.SemaphoreType.DMA((CHUNKS + 1,)),
        ],
        compiler_params=pltpu.CompilerParams(
            collective_id=0, has_side_effects=True, vmem_limit_bytes=48 << 20
        ),
    )(
        pltpu.with_memory_space_constraint(tensor.reshape(rows, N), pltpu.HBM),
        pltpu.with_memory_space_constraint(start_one.T, pltpu.HBM),
        pltpu.with_memory_space_constraint(start_two.T, pltpu.HBM),
    )
    basis_one, basis_two, core = pl.pallas_call(
        finish,
        out_shape=(
            jax.ShapeDtypeStruct((RANK, N), F32),
            jax.ShapeDtypeStruct((RANK, N), F32),
            jax.ShapeDtypeStruct((RANK // GRP * COLS, RANK), F32),
        ),
        in_specs=[vmem, vmem, vmem],
        out_specs=(hbm, hbm, hbm),
        scratch_shapes=[pltpu.SemaphoreType.DMA((3,))],
    )(*(pltpu.with_memory_space_constraint(x, pltpu.VMEM) for x in (basis_one, basis_two, core)))
    return basis_one.T, basis_two.T, core.reshape(RANK // GRP, COLS, RANK)


def solution(mesh):
    in_specs = (P("grp", "slab", None), P(), P())
    out_specs = (P(), P(), P("grp", "slab", None))
    return jax.shard_map(local, mesh=mesh, in_specs=in_specs, out_specs=out_specs, check_vma=False)
```

```python
import jax
import jax.numpy as jnp
from jax import lax
from jax.experimental import pallas as pl
from jax.experimental.pallas import tpu as pltpu
from jax.sharding import PartitionSpec as P

MESH = pl.DeviceIdType.MESH
F32 = jnp.float32
BF16 = jnp.bfloat16

N = 672
NP = 768
RANK = 96
LANES = 128
GRP = 4
COLS = 8
ROWS = N // GRP
CHUNK = 448
CHUNKS = ROWS * COLS // CHUNK
CHIPS = 64
STEP = CHUNK // COLS
BODY, TAIL = 88, 24
CORE_BODY, CORE_TAIL = 144, 48
FOLD = N // 4
OFFSETS = [(z, y, x) for z in range(4) for y in range(4) for x in range(4)]
FAR_FIRST = sorted(OFFSETS[1:], key=lambda o: -sum(min(d, 4 - d) for d in o))
NT = (((0,), (0,)), ((), ()))
NN = (((1,), (0,)), ((), ()))
TN = (((1,), (1,)), ((), ()))


def dot(a, b, dims):
    return lax.dot_general(a, b, dims, preferred_element_type=F32)


def split(x):
    high = x.astype(BF16)
    return high, (x - high.astype(F32)).astype(BF16)


def halves(x):
    return x[:, :LANES] + x[:, LANES:]


def tops(x):
    return x[:LANES] + x[LANES:]


def lane(shape):
    return lax.broadcasted_iota(jnp.int32, shape, len(shape) - 1)


def kernel(
    tensor, start_one, start_two, out_one, out_two, out_core,
    staged, starts, wide, gram, cross_part, ghigh, glow, high, low, block, exact, width, rhigh, rlow, rtilde, line, mode, given,
    packed, summed, pair, gathered, core_out, core_in,
    unit, upper, lower, inverse, stacked,
    load_sem, send_sem, recv_sem, swap_send, swap_recv,
):
    grp = lax.axis_index("grp")
    slab = lax.axis_index("slab")
    core = lax.rem(slab, 2)
    chip = grp * 16 + slab // 2

    zs = [grp] + [lax.rem(grp + d, 4) for d in range(1, 4)]
    ys = [lax.rem(slab // 8 + d, 4) * 4 for d in range(4)]
    xs = [lax.rem(slab // 2 + d, 4) for d in range(4)]
    twin = (grp, slab + 1 - 2 * core)

    def load(c):
        return pltpu.make_async_copy(
            tensor.at[pl.ds(c * CHUNK, CHUNK)], staged.at[c], load_sem.at[c]
        )

    def load_start(i):
        return pltpu.make_async_copy(
            (start_one, start_two)[i], starts.at[i], load_sem.at[CHUNKS + i]
        )

    load_start(0).start()
    for c in range(CHUNKS):
        load(c).start()
    load_start(1).start()

    barrier = pltpu.get_barrier_semaphore()
    for dz, dy, dx in FAR_FIRST:
        other = (zs[dz], (ys[dy] + xs[dx]) * 2 + core)
        pl.semaphore_signal(barrier, inc=1, device_id=other, device_id_type=MESH)
    pl.semaphore_signal(barrier, inc=1, device_id=twin, device_id_type=MESH)

    def set_block(x, rows):
        exact[0:rows, :] = x[0:rows]
        h, l = split(x)
        block[0:rows, :LANES] = h
        block[0:rows, LANES:] = l

    def pad_start(i):
        load_start(i).wait()
        wide[0:RANK, 0:N] = starts[i]
        set_block(wide[...].T, NP)

    def prepare(c):
        rows = pl.ds(c * CHUNK, CHUNK)
        x = staged[c, :, 0:640]
        y = staged[c, :, 640:N]
        high[rows, 0:640], low[rows, 0:640] = split(x)
        high[rows, 640:N], low[rows, 640:N] = split(y)
        x = jnp.sum((x * x).reshape(CHUNK // 8, 8, 640), axis=0)
        y = jnp.sum((y * y).reshape(CHUNK // 8, 8, N - 640), axis=0)
        y = jnp.concatenate([y, jnp.zeros((8, NP - N), F32)], axis=1)
        return sum((x[:, k * LANES : (k + 1) * LANES] for k in range(5)), y)

    def project(c):
        rows = pl.ds(c * CHUNK, CHUNK)
        v = block[...]
        return halves(dot(high[rows, :], v, NN) + dot(low[rows, :], v, NN))

    def product_one():
        total = None
        for c in range(CHUNKS):
            rows = pl.ds(c * CHUNK, CHUNK)
            squares = prepare(c)
            packed[0, 63] = squares if c == 0 else packed[0, 63] + squares
            yh, yl = split(project(c))
            y = jnp.concatenate([yh, yl], axis=1)
            part = tops(dot(y, high[rows, :], NT) + dot(y, low[rows, :], NT))
            total = part if total is None else total + part
        width[...] = total.T

    def gram_high():
        for i in range(3):
            a = high[:, i * 256 : (i + 1) * 256]
            gram[i * 256 : (i + 1) * 256, i * 256 :] = dot(a, high[:, i * 256 :], NT)

    def gram_low():
        for i in range(3):
            a = high[:, i * 256 : (i + 1) * 256]
            cross_part[i * 256 : (i + 1) * 256, :] = dot(a, low[...], NT)
        for i in range(3):
            for j in range(i, 3):
                a, b = slice(i * 256, (i + 1) * 256), slice(j * 256, (j + 1) * 256)
                x = gram[a, b] + cross_part[a, b] + cross_part[b, a].T
                ghigh[a, b], glow[a, b] = split(x)
                if i != j:
                    ghigh[b, a], glow[b, a] = split(x.T)

    def product_gram():
        v = block[...]
        width[0:N, :] = halves(dot(ghigh[0:N, :], v, NN) + dot(glow[0:N, :], v, NN))

    def product_two():
        v = block[0:N, :]
        z = halves(dot(rhigh[...], v, NT) + dot(rlow[...], v, NT))
        zh, zl = split(z)
        zz = jnp.concatenate([zh, zl], axis=1)
        width[0:N, :] = halves(dot(rhigh[...], zz, NN) + dot(rlow[...], zz, NN))

    def pack(r):
        tail = width[3 * FOLD : N, :]
        keep = lane((FOLD, LANES)) < RANK
        tiles = FOLD // 8
        for b in range(3):
            body = width[b * FOLD : (b + 1) * FOLD, :]
            moved = pltpu.roll(tail, RANK - 32 * b, 1)
            packed[r, b * tiles : (b + 1) * tiles] = jnp.where(keep, body, moved).reshape(
                tiles, 8, LANES
            )

    def unpack(r):
        if r == 0:
            squares = gathered[0, 63]
            trace = jnp.sum(jnp.sum(squares, axis=1, keepdims=True), axis=0, keepdims=True)
            unit[...] = jnp.broadcast_to(1.0 / trace, (8, LANES))
        scale = unit[0:1, :]
        lanes = lane((FOLD, LANES))
        tiles = FOLD // 8
        tail = jnp.zeros((FOLD, LANES), F32)
        for b in range(3):
            x = gathered[r, b * tiles : (b + 1) * tiles].reshape(FOLD, LANES) * scale
            x0 = jnp.where(lanes < RANK, x, 0.0)
            exact[b * FOLD : (b + 1) * FOLD, :] = x0
            if r % 2 == 0:
                h, l = split(x0)
                block[b * FOLD : (b + 1) * FOLD, :LANES] = h
                block[b * FOLD : (b + 1) * FOLD, LANES:] = l
            moved = pltpu.roll(x, 32 * b + 32, 1)
            tail = jnp.where((lanes >= 32 * b) & (lanes < 32 * b + 32), moved, tail)
        exact[3 * FOLD : N, :] = tail
        if r % 2 == 0:
            h, l = split(tail)
            block[3 * FOLD : N, :LANES] = h
            block[3 * FOLD : N, LANES:] = l

    def send_all(r, src, dst, stage):
        for dz, dy, dx in FAR_FIRST:
            part = ys[dy] + xs[dx]
            pltpu.make_async_remote_copy(
                src_ref=src.at[r, zs[dz] * 16 + part if stage == 0 else chip],
                dst_ref=dst.at[r, chip],
                send_sem=send_sem.at[r, stage],
                recv_sem=recv_sem.at[r, stage],
                device_id=(zs[dz], part * 2 + core),
                device_id_type=MESH,
            ).start()

    def bytes_of(ref, r, sem):
        part = ref.at[r, pl.ds(0, CHIPS - 1)]
        return pltpu.make_async_copy(part, part, sem)

    def reduce_block(r, first=None, last=None):
        pack(r)
        if r == 0:
            pl.semaphore_wait(barrier, CHIPS)
        send_all(r, packed, summed, 0)
        summed[r, pl.ds(chip, 1)] = packed[r, pl.ds(chip, 1)]
        if first is not None:
            first()
        bytes_of(summed, r, recv_sem.at[r, 0]).wait()
        parts = [summed[r, t] for t in range(CHIPS)]
        while len(parts) > 1:
            parts = [a + b for a, b in zip(parts[0::2], parts[1::2])]
        pair[r, pl.ds(core, 1)] = parts[0][None]
        twin_copy = pltpu.make_async_remote_copy(
            src_ref=pair.at[r, core],
            dst_ref=pair.at[r, core],
            send_sem=send_sem.at[r, 1],
            recv_sem=recv_sem.at[r, 1],
            device_id=twin,
            device_id_type=MESH,
        )
        twin_copy.start()
        twin_copy.wait_recv()
        gathered[r, pl.ds(chip, 1)] = (pair[r, 0] + pair[r, 1])[None]
        send_all(r, gathered, gathered, 2)
        if last is not None:
            last()
        bytes_of(gathered, r, recv_sem.at[r, 2]).wait()
        unpack(r)

    def cross_of():
        v = exact[0:N, :]
        x = lax.dot_general(v, v, NT, precision=lax.Precision.HIGHEST, preferred_element_type=F32)
        upper[...] = x[0:RANK, :]
        rows = lax.broadcasted_iota(jnp.int32, (RANK, LANES), 0)
        lower[...] = jnp.where(rows == lane((RANK, LANES)), 1.0, 0.0)

    def panel(p, tiles):
        start = pl.multiple_of(8 * p, 8)
        u = upper[pl.ds(start, 8), :]
        w = lower[pl.ds(start, 8), :]
        sub = lax.broadcasted_iota(jnp.int32, (8, LANES), 0)
        full = (8, LANES)
        cols = [jnp.broadcast_to(u[:, j : j + 1], full) for j in range(8)]
        urow, wrow, inv, elem = [], [], [], {}
        pivots = jnp.ones(full, F32)
        for j in range(8):
            pivot = jnp.broadcast_to(cols[j][j : j + 1, :], full)
            inv.append(1.0 / pivot)
            pivots = jnp.where(sub == j, pivot, pivots)
            factor = jnp.where(sub > j, cols[j] * inv[j], 0.0)
            urow.append(jnp.broadcast_to(u[j : j + 1, :], full))
            wrow.append(jnp.broadcast_to(w[j : j + 1, :], full))
            u = u - factor * urow[j]
            w = w - factor * wrow[j]
            for k in range(j + 1, 8):
                elem[j, k] = jnp.broadcast_to(cols[k][j : j + 1, :], full)
                cols[k] = cols[k] - factor * elem[j, k]
        inverse[pl.ds(start, 8), :] = w * lax.rsqrt(pivots)
        for t in tiles:
            u = upper[8 * t : 8 * t + 8, :]
            w = lower[8 * t : 8 * t + 8, :]
            cols = [jnp.broadcast_to(u[:, j : j + 1], full) for j in range(8)]
            for j in range(8):
                factor = cols[j] * inv[j]
                u = u - factor * urow[j]
                w = w - factor * wrow[j]
                for k in range(j + 1, 8):
                    cols[k] = cols[k] - factor * elem[j, k]
            upper[8 * t : 8 * t + 8, :] = pltpu.roll(u, LANES - 8, 1)
            lower[8 * t : 8 * t + 8, :] = w

    def panels(first, last):
        def step(p, carry):
            panel(p, range(first + 1, 12))
            return carry

        lax.fori_loop(first, last, step, 0)

    def stack():
        h, l = split(inverse[...])
        stacked[:LANES, :] = h
        stacked[LANES:, :] = l

    def factor_start():
        cross_of()
        panels(0, 4)

    def factor_end():
        panels(4, 8)
        panels(8, 12)

    def basis():
        return lax.dot_general(
            inverse[0:RANK, :], exact[0:N, :], TN,
            precision=lax.Precision.HIGHEST, preferred_element_type=F32,
        )

    def apply(rows):
        return lax.dot_general(exact[rows, :], inverse[...], TN, precision=lax.Precision.HIGHEST, preferred_element_type=F32)

    packed[1:, 63] = jnp.zeros((3, 8, LANES), F32)
    high[:, 640:NP] = jnp.zeros((high.shape[0], LANES), BF16)
    low[:, 640:NP] = jnp.zeros((low.shape[0], LANES), BF16)
    inverse[...] = jnp.zeros_like(inverse)
    wide[...] = jnp.zeros_like(wide)
    pad_start(0)
    for c in range(CHUNKS):
        load(c).wait()
    product_one()
    reduce_block(0, gram_high, gram_low)
    product_gram()
    reduce_block(1, factor_start, factor_end)
    set_block(apply(slice(0, N)), N)

    def fold(target, body, tail):
        keep = lane((tail, LANES)) < RANK
        end = line[body : body + tail, :]
        for b in range(3):
            rows = slice(b * tail, (b + 1) * tail)
            target[rows] = jnp.where(keep, line[rows, :], pltpu.roll(end, RANK - 32 * b, 1))
        if body > 3 * tail:
            target[3 * tail : body] = line[3 * tail : body, :]

    def unfold(source, start, body, tail):
        lanes = lane((tail, LANES))
        end = jnp.zeros((tail, LANES), F32)
        for b in range(3):
            x = source[b * tail : (b + 1) * tail]
            line[start + b * tail : start + (b + 1) * tail, :] = jnp.where(lanes < RANK, x, 0.0)
            inside = (lanes >= 32 * b) & (lanes < 32 * b + 32)
            end = jnp.where(inside, pltpu.roll(x, 32 * b + 32, 1), end)
        if body > 3 * tail:
            line[start + 3 * tail : start + body, :] = source[3 * tail : body]
        line[start + body : start + body + tail, :] = end

    def swap(src, dst, k, r):
        g = lax.rem(grp + k, GRP)
        return pltpu.make_async_remote_copy(
            src_ref=src(g),
            dst_ref=dst,
            send_sem=swap_send.at[r],
            recv_sem=swap_recv.at[r],
            device_id=(g, slab),
            device_id_type=MESH,
        )

    def three(ref, sem):
        part = ref.at[pl.ds(0, GRP - 1)]
        return pltpu.make_async_copy(part, part, sem)

    for c in range(CHUNKS):
        rtilde[c * CHUNK : (c + 1) * CHUNK, :] = project(c)
        for g in range(GRP):
            for m in range(2):
                line[m * STEP : (m + 1) * STEP, :] = rtilde[
                    pl.ds(c * CHUNK + 2 * g + m, STEP, stride=COLS), :
                ]
            fold(mode.at[c, g], BODY, TAIL)
        for k in (2, 1, 3):
            swap(lambda g: mode.at[c, g], given.at[c, grp], k, c).start()
        given[c, pl.ds(grp, 1)] = mode[c, pl.ds(grp, 1)]
    factor_start()
    factor_end()
    stack()
    out_one[...] = basis()
    width[N:NP, :] = jnp.zeros((NP - N, LANES), F32)
    pad_start(1)
    f = stacked[...]
    for c in range(CHUNKS):
        three(given.at[c], swap_recv.at[c]).wait()
        size = 2 * STEP
        for g in range(GRP):
            unfold(given.at[c, g], g * size, BODY, TAIL)
        h, l = split(line[...])
        y = halves(dot(h, f, TN) + dot(l, f, TN))
        for g in range(GRP):
            rows = slice(g * ROWS + c * STEP, g * ROWS + (c + 1) * STEP)
            for m in range(2):
                h, l = split(y[g * size + m * STEP : g * size + (m + 1) * STEP])
                rhigh[rows, m * LANES : (m + 1) * LANES] = h
                rlow[rows, m * LANES : (m + 1) * LANES] = l
    for c in range(CHUNKS):
        three(mode.at[c], swap_send.at[c]).wait()

    product_two()
    reduce_block(2)
    product_two()
    reduce_block(3, factor_start, factor_end)
    set_block(apply(slice(0, N)), N)
    v = block[0:N, :]
    partial = tops(dot(v, rhigh[...], NT) + dot(v, rlow[...], NT))
    for m in range(2):
        line[m * RANK : (m + 1) * RANK, :] = partial[0:RANK, m * LANES : (m + 1) * LANES]
    fold(core_out, CORE_BODY, CORE_TAIL)
    for k in (2, 1, 3):
        swap(lambda g: core_out, core_in.at[grp], k, CHUNKS).start()
    core_in[pl.ds(grp, 1)] = core_out[...][None]
    factor_start()
    factor_end()
    out_two[...] = basis()
    mine = inverse[pl.ds(pl.multiple_of(grp * 24, 8), 24), 0:RANK]
    three(core_in, swap_recv.at[CHUNKS]).wait()
    for g in range(GRP):
        unfold(core_in.at[g], 0, CORE_BODY, CORE_TAIL)
        x = jnp.concatenate([line[0:RANK, :], line[RANK : 2 * RANK, :]], axis=1)
        y = jnp.dot(mine, x, precision=lax.Precision.HIGHEST)
        for m in range(2):
            out_core[pl.ds(2 * g + m, 24, stride=COLS), :] = y[:, m * LANES : m * LANES + RANK]
    for k in range(1, GRP):
        pltpu.make_async_copy(core_out, core_out, swap_send.at[CHUNKS]).wait()
    for r in range(4):
        bytes_of(packed, r, send_sem.at[r, 0]).wait()
        pltpu.make_async_copy(pair.at[r, 0], pair.at[r, 0], send_sem.at[r, 1]).wait()
        bytes_of(gathered, r, send_sem.at[r, 2]).wait()


def finish(one, two, core, out_one, out_two, out_core, sems):
    pairs = ((one, out_one), (two, out_two), (core, out_core))
    copies = [pltpu.make_async_copy(a, b, sems.at[i]) for i, (a, b) in enumerate(pairs)]
    for copy in copies:
        copy.start()
    for copy in copies:
        copy.wait()


def local(tensor, start_one, start_two):
    rows = ROWS * COLS
    vmem = pl.BlockSpec(memory_space=pltpu.VMEM)
    hbm = pl.BlockSpec(memory_space=pltpu.HBM)
    basis_one, basis_two, core = pl.pallas_call(
        kernel,
        out_shape=(
            jax.ShapeDtypeStruct((RANK, N), F32),
            jax.ShapeDtypeStruct((RANK, N), F32),
            jax.ShapeDtypeStruct((RANK // GRP * COLS, RANK), F32),
        ),
        in_specs=[hbm, hbm, hbm],
        out_specs=(vmem, vmem, vmem),
        scratch_shapes=[
            pltpu.VMEM((CHUNKS, CHUNK, N), F32),
            pltpu.VMEM((2, RANK, N), F32),
            pltpu.VMEM((LANES, NP), F32),
            pltpu.VMEM((NP, NP), F32),
            pltpu.VMEM((NP, NP), F32),
            pltpu.VMEM((NP, NP), BF16),
            pltpu.VMEM((NP, NP), BF16),
            pltpu.VMEM((rows, NP), BF16),
            pltpu.VMEM((rows, NP), BF16),
            pltpu.VMEM((NP, 2 * LANES), BF16),
            pltpu.VMEM((NP, LANES), F32),
            pltpu.VMEM((NP, LANES), F32),
            pltpu.VMEM((N, 2 * LANES), BF16),
            pltpu.VMEM((N, 2 * LANES), BF16),
            pltpu.VMEM((rows, LANES), F32),
            pltpu.VMEM((CHUNK, LANES), F32),
            pltpu.VMEM((CHUNKS, GRP, BODY, LANES), F32),
            pltpu.VMEM((CHUNKS, GRP, BODY, LANES), F32),
            pltpu.VMEM((4, CHIPS, 8, LANES), F32),
            pltpu.VMEM((4, CHIPS, 8, LANES), F32),
            pltpu.VMEM((4, 2, 8, LANES), F32),
            pltpu.VMEM((4, CHIPS, 8, LANES), F32),
            pltpu.VMEM((CORE_BODY, LANES), F32),
            pltpu.VMEM((GRP, CORE_BODY, LANES), F32),
            pltpu.VMEM((8, LANES), F32),
            pltpu.VMEM((RANK, LANES), F32),
            pltpu.VMEM((RANK, LANES), F32),
            pltpu.VMEM((LANES, LANES), F32),
            pltpu.VMEM((2 * LANES, LANES), BF16),
            pltpu.SemaphoreType.DMA((CHUNKS + 2,)),
            pltpu.SemaphoreType.DMA((4, 3)),
            pltpu.SemaphoreType.DMA((4, 3)),
            pltpu.SemaphoreType.DMA((CHUNKS + 1,)),
            pltpu.SemaphoreType.DMA((CHUNKS + 1,)),
        ],
        compiler_params=pltpu.CompilerParams(
            collective_id=0, has_side_effects=True, vmem_limit_bytes=48 << 20
        ),
    )(
        pltpu.with_memory_space_constraint(tensor.reshape(rows, N), pltpu.HBM),
        pltpu.with_memory_space_constraint(start_one.T, pltpu.HBM),
        pltpu.with_memory_space_constraint(start_two.T, pltpu.HBM),
    )
    basis_one, basis_two, core = pl.pallas_call(
        finish,
        out_shape=(
            jax.ShapeDtypeStruct((RANK, N), F32),
            jax.ShapeDtypeStruct((RANK, N), F32),
            jax.ShapeDtypeStruct((RANK // GRP * COLS, RANK), F32),
        ),
        in_specs=[vmem, vmem, vmem],
        out_specs=(hbm, hbm, hbm),
        scratch_shapes=[pltpu.SemaphoreType.DMA((3,))],
    )(*(pltpu.with_memory_space_constraint(x, pltpu.VMEM) for x in (basis_one, basis_two, core)))
    return basis_one.T, basis_two.T, core.reshape(RANK // GRP, COLS, RANK)


def solution(mesh):
    in_specs = (P("grp", "slab", None), P(), P())
    out_specs = (P(), P(), P("grp", "slab", None))
    return jax.shard_map(local, mesh=mesh, in_specs=in_specs, out_specs=out_specs, check_vma=False)
```

```python
import jax
import jax.numpy as jnp
from jax import lax
from jax.experimental import pallas as pl
from jax.experimental.pallas import tpu as pltpu
from jax.sharding import PartitionSpec as P

MESH = pl.DeviceIdType.MESH
F32 = jnp.float32
BF16 = jnp.bfloat16

N = 672
NP = 768
RANK = 96
LANES = 128
GRP = 4
COLS = 8
ROWS = N // GRP
CHUNK = 448
CHUNKS = ROWS * COLS // CHUNK
CHIPS = 64
STEP = CHUNK // COLS
BODY, TAIL = 88, 24
CORE_BODY, CORE_TAIL = 144, 48
FOLD = N // 4
OFFSETS = [(z, y, x) for z in range(4) for y in range(4) for x in range(4)]
FAR_FIRST = sorted(OFFSETS[1:], key=lambda o: -sum(min(d, 4 - d) for d in o))
NT = (((0,), (0,)), ((), ()))
NN = (((1,), (0,)), ((), ()))
TN = (((1,), (1,)), ((), ()))


def dot(a, b, dims):
    return lax.dot_general(a, b, dims, preferred_element_type=F32)


def split(x):
    high = x.astype(BF16)
    return high, (x - high.astype(F32)).astype(BF16)


def halves(x):
    return x[:, :LANES] + x[:, LANES:]


def tops(x):
    return x[:LANES] + x[LANES:]


def lane(shape):
    return lax.broadcasted_iota(jnp.int32, shape, len(shape) - 1)


def kernel(
    tensor, start_one, start_two, out_one, out_two, out_core,
    staged, starts, wide, gram, gram_in, cross_part, ghigh, glow, high, low, block, exact, width, rhigh, rlow, rtilde, line, mode, given,
    packed, summed, pair, gathered, core_out, core_in,
    unit, upper, lower, inverse, stacked,
    load_sem, send_sem, recv_sem, swap_send, swap_recv, gram_send, gram_recv,
):
    grp = lax.axis_index("grp")
    slab = lax.axis_index("slab")
    core = lax.rem(slab, 2)
    chip = grp * 16 + slab // 2

    zs = [grp] + [lax.rem(grp + d, 4) for d in range(1, 4)]
    ys = [lax.rem(slab // 8 + d, 4) * 4 for d in range(4)]
    xs = [lax.rem(slab // 2 + d, 4) for d in range(4)]
    twin = (grp, slab + 1 - 2 * core)

    def load(c):
        return pltpu.make_async_copy(
            tensor.at[pl.ds(c * CHUNK, CHUNK)], staged.at[c], load_sem.at[c]
        )

    def load_start(i):
        return pltpu.make_async_copy(
            (start_one, start_two)[i], starts.at[i], load_sem.at[CHUNKS + i]
        )

    load_start(0).start()
    for c in range(CHUNKS):
        load(c).start()
    load_start(1).start()

    barrier = pltpu.get_barrier_semaphore()
    for dz, dy, dx in FAR_FIRST:
        other = (zs[dz], (ys[dy] + xs[dx]) * 2 + core)
        pl.semaphore_signal(barrier, inc=1, device_id=other, device_id_type=MESH)
    pl.semaphore_signal(barrier, inc=1, device_id=twin, device_id_type=MESH)

    def set_block(x, rows):
        exact[0:rows, :] = x[0:rows]
        h, l = split(x)
        block[0:rows, :LANES] = h
        block[0:rows, LANES:] = l

    def pad_start(i):
        load_start(i).wait()
        wide[0:RANK, 0:N] = starts[i]
        set_block(wide[...].T, NP)

    def prepare(c):
        rows = pl.ds(c * CHUNK, CHUNK)
        x = staged[c, :, 0:640]
        y = staged[c, :, 640:N]
        high[rows, 0:640], low[rows, 0:640] = split(x)
        high[rows, 640:N], low[rows, 640:N] = split(y)
        x = jnp.sum((x * x).reshape(CHUNK // 8, 8, 640), axis=0)
        y = jnp.sum((y * y).reshape(CHUNK // 8, 8, N - 640), axis=0)
        y = jnp.concatenate([y, jnp.zeros((8, NP - N), F32)], axis=1)
        return sum((x[:, k * LANES : (k + 1) * LANES] for k in range(5)), y)

    def project(c):
        rows = pl.ds(c * CHUNK, CHUNK)
        v = block[...]
        return halves(dot(high[rows, :], v, NN) + dot(low[rows, :], v, NN))

    def product_one():
        total = None
        for c in range(CHUNKS):
            rows = pl.ds(c * CHUNK, CHUNK)
            squares = prepare(c)
            packed[0, 63] = squares if c == 0 else packed[0, 63] + squares
            yh, yl = split(project(c))
            y = jnp.concatenate([yh, yl], axis=1)
            part = tops(dot(y, high[rows, :], NT) + dot(y, low[rows, :], NT))
            total = part if total is None else total + part
        width[...] = total.T

    def gram_block(n, i, right, start):
        rows = slice(i * 256, (i + 1) * 256)
        if n == 0:
            return dot(high[:, rows], right[:, start:], NT)
        return dot(rhigh[rows, :], right[start:, :], TN)

    def gram_copy(n, i):
        part = (n, pl.ds(i * 256, 256), pl.ds(i * 256, NP - i * 256))
        return pltpu.make_async_remote_copy(
            src_ref=gram.at[part],
            dst_ref=gram_in.at[part],
            send_sem=gram_send.at[n, i],
            recv_sem=gram_recv.at[n, i],
            device_id=twin,
            device_id_type=MESH,
        )

    def gram_start(n):
        for i in range(3):
            rows = slice(i * 256, (i + 1) * 256)
            gram[n, rows, i * 256 :] = gram_block(n, i, (high, rhigh)[n], i * 256)
        for i in range(3):
            rows = slice(i * 256, (i + 1) * 256)
            cross_part[rows, :] = gram_block(n, i, (low, rlow)[n], 0)
        for i in range(3):
            for j in range(i, 3):
                a, b = slice(i * 256, (i + 1) * 256), slice(j * 256, (j + 1) * 256)
                gram[n, a, b] = gram[n, a, b] + cross_part[a, b] + cross_part[b, a].T
            gram_copy(n, i).start()

    def gram_pair(n):
        for i in range(3):
            gram_copy(n, i).wait_recv()
            for j in range(i, 3):
                a, b = slice(i * 256, (i + 1) * 256), slice(j * 256, (j + 1) * 256)
                x = gram[n, a, b] + gram_in[n, a, b]
                ghigh[a, b], glow[a, b] = split(x)
                if i != j:
                    ghigh[b, a], glow[b, a] = split(x.T)

    def product_gram():
        v = block[...]
        width[0:N, :] = halves(dot(ghigh[0:N, :], v, NN) + dot(glow[0:N, :], v, NN))

    def product_two():
        v = block[0:N, :]
        z = halves(dot(rhigh[0:N, :], v, NT) + dot(rlow[0:N, :], v, NT))
        zh, zl = split(z)
        zz = jnp.concatenate([zh, zl], axis=1)
        width[0:N, :] = halves(dot(rhigh[0:N, :], zz, NN) + dot(rlow[0:N, :], zz, NN))

    def pack(r):
        tail = width[3 * FOLD : N, :]
        keep = lane((FOLD, LANES)) < RANK
        tiles = FOLD // 8
        for b in range(3):
            body = width[b * FOLD : (b + 1) * FOLD, :]
            moved = pltpu.roll(tail, RANK - 32 * b, 1)
            packed[r, b * tiles : (b + 1) * tiles] = jnp.where(keep, body, moved).reshape(
                tiles, 8, LANES
            )

    def unpack(r):
        if r == 0:
            squares = gathered[0, 63]
            trace = jnp.sum(jnp.sum(squares, axis=1, keepdims=True), axis=0, keepdims=True)
            unit[...] = jnp.broadcast_to(1.0 / trace, (8, LANES))
        scale = unit[0:1, :]
        lanes = lane((FOLD, LANES))
        tiles = FOLD // 8
        tail = jnp.zeros((FOLD, LANES), F32)
        for b in range(3):
            x = gathered[r, b * tiles : (b + 1) * tiles].reshape(FOLD, LANES) * scale
            x0 = jnp.where(lanes < RANK, x, 0.0)
            exact[b * FOLD : (b + 1) * FOLD, :] = x0
            if r % 2 == 0:
                h, l = split(x0)
                block[b * FOLD : (b + 1) * FOLD, :LANES] = h
                block[b * FOLD : (b + 1) * FOLD, LANES:] = l
            moved = pltpu.roll(x, 32 * b + 32, 1)
            tail = jnp.where((lanes >= 32 * b) & (lanes < 32 * b + 32), moved, tail)
        exact[3 * FOLD : N, :] = tail
        if r % 2 == 0:
            h, l = split(tail)
            block[3 * FOLD : N, :LANES] = h
            block[3 * FOLD : N, LANES:] = l

    def send_all(r, src, dst, stage):
        for dz, dy, dx in FAR_FIRST:
            part = ys[dy] + xs[dx]
            pltpu.make_async_remote_copy(
                src_ref=src.at[r, zs[dz] * 16 + part if stage == 0 else chip],
                dst_ref=dst.at[r, chip],
                send_sem=send_sem.at[r, stage],
                recv_sem=recv_sem.at[r, stage],
                device_id=(zs[dz], part * 2 + core),
                device_id_type=MESH,
            ).start()

    def bytes_of(ref, r, sem):
        part = ref.at[r, pl.ds(0, CHIPS - 1)]
        return pltpu.make_async_copy(part, part, sem)

    def reduce_block(r, first=None, last=None):
        pack(r)
        if r == 0:
            pl.semaphore_wait(barrier, CHIPS)
        send_all(r, packed, summed, 0)
        summed[r, pl.ds(chip, 1)] = packed[r, pl.ds(chip, 1)]
        if first is not None:
            first()
        bytes_of(summed, r, recv_sem.at[r, 0]).wait()
        parts = [summed[r, t] for t in range(CHIPS)]
        while len(parts) > 1:
            parts = [a + b for a, b in zip(parts[0::2], parts[1::2])]
        total = parts[0]
        if r % 2 == 0:
            pair[r, pl.ds(core, 1)] = total[None]
            twin_copy = pltpu.make_async_remote_copy(
                src_ref=pair.at[r, core],
                dst_ref=pair.at[r, core],
                send_sem=send_sem.at[r, 1],
                recv_sem=recv_sem.at[r, 1],
                device_id=twin,
                device_id_type=MESH,
            )
            twin_copy.start()
            twin_copy.wait_recv()
            total = pair[r, 0] + pair[r, 1]
        gathered[r, pl.ds(chip, 1)] = total[None]
        send_all(r, gathered, gathered, 2)
        if last is not None:
            last()
        bytes_of(gathered, r, recv_sem.at[r, 2]).wait()
        unpack(r)

    def cross_of():
        v = exact[0:N, :]
        x = lax.dot_general(v, v, NT, precision=lax.Precision.HIGHEST, preferred_element_type=F32)
        upper[...] = x[0:RANK, :]
        rows = lax.broadcasted_iota(jnp.int32, (RANK, LANES), 0)
        lower[...] = jnp.where(rows == lane((RANK, LANES)), 1.0, 0.0)

    def panel(p, tiles):
        start = pl.multiple_of(8 * p, 8)
        u = upper[pl.ds(start, 8), :]
        w = lower[pl.ds(start, 8), :]
        sub = lax.broadcasted_iota(jnp.int32, (8, LANES), 0)
        full = (8, LANES)
        cols = [jnp.broadcast_to(u[:, j : j + 1], full) for j in range(8)]
        urow, wrow, inv, elem = [], [], [], {}
        pivots = jnp.ones(full, F32)
        for j in range(8):
            pivot = jnp.broadcast_to(cols[j][j : j + 1, :], full)
            inv.append(1.0 / pivot)
            pivots = jnp.where(sub == j, pivot, pivots)
            factor = jnp.where(sub > j, cols[j] * inv[j], 0.0)
            urow.append(jnp.broadcast_to(u[j : j + 1, :], full))
            wrow.append(jnp.broadcast_to(w[j : j + 1, :], full))
            u = u - factor * urow[j]
            w = w - factor * wrow[j]
            for k in range(j + 1, 8):
                elem[j, k] = jnp.broadcast_to(cols[k][j : j + 1, :], full)
                cols[k] = cols[k] - factor * elem[j, k]
        inverse[pl.ds(start, 8), :] = w * lax.rsqrt(pivots)
        for t in tiles:
            u = upper[8 * t : 8 * t + 8, :]
            w = lower[8 * t : 8 * t + 8, :]
            cols = [jnp.broadcast_to(u[:, j : j + 1], full) for j in range(8)]
            for j in range(8):
                factor = cols[j] * inv[j]
                u = u - factor * urow[j]
                w = w - factor * wrow[j]
                for k in range(j + 1, 8):
                    cols[k] = cols[k] - factor * elem[j, k]
            upper[8 * t : 8 * t + 8, :] = pltpu.roll(u, LANES - 8, 1)
            lower[8 * t : 8 * t + 8, :] = w

    def panels(first, last):
        def step(p, carry):
            panel(p, range(first + 1, 12))
            return carry

        lax.fori_loop(first, last, step, 0)

    def stack():
        h, l = split(inverse[...])
        stacked[:LANES, :] = h
        stacked[LANES:, :] = l

    def factor_start():
        cross_of()
        panels(0, 4)

    def factor_end():
        panels(4, 8)
        panels(8, 12)

    def basis():
        return lax.dot_general(
            inverse[0:RANK, :], exact[0:N, :], TN,
            precision=lax.Precision.HIGHEST, preferred_element_type=F32,
        )

    def apply(rows):
        return lax.dot_general(exact[rows, :], inverse[...], TN, precision=lax.Precision.HIGHEST, preferred_element_type=F32)

    packed[1:, 63] = jnp.zeros((3, 8, LANES), F32)
    high[:, 640:NP] = jnp.zeros((high.shape[0], LANES), BF16)
    low[:, 640:NP] = jnp.zeros((low.shape[0], LANES), BF16)
    inverse[...] = jnp.zeros_like(inverse)
    rhigh[N:NP, :] = jnp.zeros((NP - N, 2 * LANES), BF16)
    rlow[N:NP, :] = jnp.zeros((NP - N, 2 * LANES), BF16)
    wide[...] = jnp.zeros_like(wide)
    pad_start(0)
    for c in range(CHUNKS):
        load(c).wait()
    product_one()
    reduce_block(0, lambda: gram_start(0), lambda: gram_pair(0))
    product_gram()
    reduce_block(1, factor_start, factor_end)
    set_block(apply(slice(0, N)), N)

    def fold(target, body, tail):
        keep = lane((tail, LANES)) < RANK
        end = line[body : body + tail, :]
        for b in range(3):
            rows = slice(b * tail, (b + 1) * tail)
            target[rows] = jnp.where(keep, line[rows, :], pltpu.roll(end, RANK - 32 * b, 1))
        if body > 3 * tail:
            target[3 * tail : body] = line[3 * tail : body, :]

    def unfold(source, start, body, tail):
        lanes = lane((tail, LANES))
        end = jnp.zeros((tail, LANES), F32)
        for b in range(3):
            x = source[b * tail : (b + 1) * tail]
            line[start + b * tail : start + (b + 1) * tail, :] = jnp.where(lanes < RANK, x, 0.0)
            inside = (lanes >= 32 * b) & (lanes < 32 * b + 32)
            end = jnp.where(inside, pltpu.roll(x, 32 * b + 32, 1), end)
        if body > 3 * tail:
            line[start + 3 * tail : start + body, :] = source[3 * tail : body]
        line[start + body : start + body + tail, :] = end

    def swap(src, dst, k, r):
        g = lax.rem(grp + k, GRP)
        return pltpu.make_async_remote_copy(
            src_ref=src(g),
            dst_ref=dst,
            send_sem=swap_send.at[r],
            recv_sem=swap_recv.at[r],
            device_id=(g, slab),
            device_id_type=MESH,
        )

    def three(ref, sem):
        part = ref.at[pl.ds(0, GRP - 1)]
        return pltpu.make_async_copy(part, part, sem)

    for c in range(CHUNKS):
        rtilde[c * CHUNK : (c + 1) * CHUNK, :] = project(c)
        for g in range(GRP):
            for m in range(2):
                line[m * STEP : (m + 1) * STEP, :] = rtilde[
                    pl.ds(c * CHUNK + 2 * g + m, STEP, stride=COLS), :
                ]
            fold(mode.at[c, g], BODY, TAIL)
        for k in (2, 1, 3):
            swap(lambda g: mode.at[c, g], given.at[c, grp], k, c).start()
        given[c, pl.ds(grp, 1)] = mode[c, pl.ds(grp, 1)]
    factor_start()
    factor_end()
    stack()
    out_one[...] = basis()
    width[N:NP, :] = jnp.zeros((NP - N, LANES), F32)
    pad_start(1)
    f = stacked[...]
    for c in range(CHUNKS):
        three(given.at[c], swap_recv.at[c]).wait()
        size = 2 * STEP
        for g in range(GRP):
            unfold(given.at[c, g], g * size, BODY, TAIL)
        h, l = split(line[...])
        y = halves(dot(h, f, TN) + dot(l, f, TN))
        for g in range(GRP):
            rows = slice(g * ROWS + c * STEP, g * ROWS + (c + 1) * STEP)
            for m in range(2):
                h, l = split(y[g * size + m * STEP : g * size + (m + 1) * STEP])
                rhigh[rows, m * LANES : (m + 1) * LANES] = h
                rlow[rows, m * LANES : (m + 1) * LANES] = l
    for c in range(CHUNKS):
        three(mode.at[c], swap_send.at[c]).wait()

    product_two()
    reduce_block(2, lambda: gram_start(1), lambda: gram_pair(1))
    product_gram()
    reduce_block(3, factor_start, factor_end)
    set_block(apply(slice(0, N)), N)
    v = block[0:N, :]
    partial = tops(dot(v, rhigh[0:N, :], NT) + dot(v, rlow[0:N, :], NT))
    for m in range(2):
        line[m * RANK : (m + 1) * RANK, :] = partial[0:RANK, m * LANES : (m + 1) * LANES]
    fold(core_out, CORE_BODY, CORE_TAIL)
    for k in (2, 1, 3):
        swap(lambda g: core_out, core_in.at[grp], k, CHUNKS).start()
    core_in[pl.ds(grp, 1)] = core_out[...][None]
    factor_start()
    factor_end()
    out_two[...] = basis()
    mine = inverse[pl.ds(pl.multiple_of(grp * 24, 8), 24), 0:RANK]
    three(core_in, swap_recv.at[CHUNKS]).wait()
    for g in range(GRP):
        unfold(core_in.at[g], 0, CORE_BODY, CORE_TAIL)
        x = jnp.concatenate([line[0:RANK, :], line[RANK : 2 * RANK, :]], axis=1)
        y = jnp.dot(mine, x, precision=lax.Precision.HIGHEST)
        for m in range(2):
            out_core[pl.ds(2 * g + m, 24, stride=COLS), :] = y[:, m * LANES : m * LANES + RANK]
    for k in range(1, GRP):
        pltpu.make_async_copy(core_out, core_out, swap_send.at[CHUNKS]).wait()
    for i in range(3):
        gram_copy(0, i).wait_send()
        gram_copy(1, i).wait_send()
    for r in range(4):
        bytes_of(packed, r, send_sem.at[r, 0]).wait()
        if r % 2 == 0:
            pltpu.make_async_copy(pair.at[r, 0], pair.at[r, 0], send_sem.at[r, 1]).wait()
        bytes_of(gathered, r, send_sem.at[r, 2]).wait()


def finish(one, two, core, out_one, out_two, out_core, sems):
    pairs = ((one, out_one), (two, out_two), (core, out_core))
    copies = [pltpu.make_async_copy(a, b, sems.at[i]) for i, (a, b) in enumerate(pairs)]
    for copy in copies:
        copy.start()
    for copy in copies:
        copy.wait()


def local(tensor, start_one, start_two):
    rows = ROWS * COLS
    vmem = pl.BlockSpec(memory_space=pltpu.VMEM)
    hbm = pl.BlockSpec(memory_space=pltpu.HBM)
    basis_one, basis_two, core = pl.pallas_call(
        kernel,
        out_shape=(
            jax.ShapeDtypeStruct((RANK, N), F32),
            jax.ShapeDtypeStruct((RANK, N), F32),
            jax.ShapeDtypeStruct((RANK // GRP * COLS, RANK), F32),
        ),
        in_specs=[hbm, hbm, hbm],
        out_specs=(vmem, vmem, vmem),
        scratch_shapes=[
            pltpu.VMEM((CHUNKS, CHUNK, N), F32),
            pltpu.VMEM((2, RANK, N), F32),
            pltpu.VMEM((LANES, NP), F32),
            pltpu.VMEM((2, NP, NP), F32),
            pltpu.VMEM((2, NP, NP), F32),
            pltpu.VMEM((NP, NP), F32),
            pltpu.VMEM((NP, NP), BF16),
            pltpu.VMEM((NP, NP), BF16),
            pltpu.VMEM((rows, NP), BF16),
            pltpu.VMEM((rows, NP), BF16),
            pltpu.VMEM((NP, 2 * LANES), BF16),
            pltpu.VMEM((NP, LANES), F32),
            pltpu.VMEM((NP, LANES), F32),
            pltpu.VMEM((NP, 2 * LANES), BF16),
            pltpu.VMEM((NP, 2 * LANES), BF16),
            pltpu.VMEM((rows, LANES), F32),
            pltpu.VMEM((CHUNK, LANES), F32),
            pltpu.VMEM((CHUNKS, GRP, BODY, LANES), F32),
            pltpu.VMEM((CHUNKS, GRP, BODY, LANES), F32),
            pltpu.VMEM((4, CHIPS, 8, LANES), F32),
            pltpu.VMEM((4, CHIPS, 8, LANES), F32),
            pltpu.VMEM((4, 2, 8, LANES), F32),
            pltpu.VMEM((4, CHIPS, 8, LANES), F32),
            pltpu.VMEM((CORE_BODY, LANES), F32),
            pltpu.VMEM((GRP, CORE_BODY, LANES), F32),
            pltpu.VMEM((8, LANES), F32),
            pltpu.VMEM((RANK, LANES), F32),
            pltpu.VMEM((RANK, LANES), F32),
            pltpu.VMEM((LANES, LANES), F32),
            pltpu.VMEM((2 * LANES, LANES), BF16),
            pltpu.SemaphoreType.DMA((CHUNKS + 2,)),
            pltpu.SemaphoreType.DMA((4, 3)),
            pltpu.SemaphoreType.DMA((4, 3)),
            pltpu.SemaphoreType.DMA((CHUNKS + 1,)),
            pltpu.SemaphoreType.DMA((CHUNKS + 1,)),
            pltpu.SemaphoreType.DMA((2, 3)),
            pltpu.SemaphoreType.DMA((2, 3)),
        ],
        compiler_params=pltpu.CompilerParams(
            collective_id=0, has_side_effects=True, vmem_limit_bytes=48 << 20
        ),
    )(
        pltpu.with_memory_space_constraint(tensor.reshape(rows, N), pltpu.HBM),
        pltpu.with_memory_space_constraint(start_one.T, pltpu.HBM),
        pltpu.with_memory_space_constraint(start_two.T, pltpu.HBM),
    )
    basis_one, basis_two, core = pl.pallas_call(
        finish,
        out_shape=(
            jax.ShapeDtypeStruct((RANK, N), F32),
            jax.ShapeDtypeStruct((RANK, N), F32),
            jax.ShapeDtypeStruct((RANK // GRP * COLS, RANK), F32),
        ),
        in_specs=[vmem, vmem, vmem],
        out_specs=(hbm, hbm, hbm),
        scratch_shapes=[pltpu.SemaphoreType.DMA((3,))],
    )(*(pltpu.with_memory_space_constraint(x, pltpu.VMEM) for x in (basis_one, basis_two, core)))
    return basis_one.T, basis_two.T, core.reshape(RANK // GRP, COLS, RANK)


def solution(mesh):
    in_specs = (P("grp", "slab", None), P(), P())
    out_specs = (P(), P(), P("grp", "slab", None))
    return jax.shard_map(local, mesh=mesh, in_specs=in_specs, out_specs=out_specs, check_vma=False)
```

```python
import jax
import jax.numpy as jnp
from jax import lax
from jax.experimental import pallas as pl
from jax.experimental.pallas import tpu as pltpu
from jax.sharding import PartitionSpec as P

MESH = pl.DeviceIdType.MESH
F32 = jnp.float32
BF16 = jnp.bfloat16

N = 672
NP = 768
RANK = 96
LANES = 128
GRP = 4
COLS = 8
ROWS = N // GRP
CHUNK = 448
CHUNKS = ROWS * COLS // CHUNK
CHIPS = 64
STEP = CHUNK // COLS
BODY, TAIL = 88, 24
CORE_BODY, CORE_TAIL = 144, 48
FOLD = N // 4
OFFSETS = [(z, y, x) for z in range(4) for y in range(4) for x in range(4)]
FAR_FIRST = sorted(OFFSETS[1:], key=lambda o: -sum(min(d, 4 - d) for d in o))
NT = (((0,), (0,)), ((), ()))
NN = (((1,), (0,)), ((), ()))
TN = (((1,), (1,)), ((), ()))


def dot(a, b, dims):
    return lax.dot_general(a, b, dims, preferred_element_type=F32)


def split(x):
    high = x.astype(BF16)
    return high, (x - high.astype(F32)).astype(BF16)


def halves(x):
    return x[:, :LANES] + x[:, LANES:]


def tops(x):
    return x[:LANES] + x[LANES:]


def lane(shape):
    return lax.broadcasted_iota(jnp.int32, shape, len(shape) - 1)


def kernel(
    tensor, start_one, start_two, out_one, out_two, out_core,
    staged, starts, wide, second, gram, gram_in, cross_part, ghigh, glow, high, low, block, exact, width, rhigh, rlow, rtilde, line, mode, given,
    packed, summed, pair, gathered, core_out, core_in,
    unit, upper, lower, inverse, stacked,
    load_sem, send_sem, recv_sem, swap_send, swap_recv, gram_send, gram_recv,
):
    grp = lax.axis_index("grp")
    slab = lax.axis_index("slab")
    core = lax.rem(slab, 2)
    chip = grp * 16 + slab // 2

    zs = [grp] + [lax.rem(grp + d, 4) for d in range(1, 4)]
    ys = [lax.rem(slab // 8 + d, 4) * 4 for d in range(4)]
    xs = [lax.rem(slab // 2 + d, 4) for d in range(4)]
    twin = (grp, slab + 1 - 2 * core)

    def load(c):
        return pltpu.make_async_copy(
            tensor.at[pl.ds(c * CHUNK, CHUNK)], staged.at[c], load_sem.at[c]
        )

    def load_start(i):
        return pltpu.make_async_copy(
            (start_one, start_two)[i], starts.at[i], load_sem.at[CHUNKS + i]
        )

    barrier = pltpu.get_barrier_semaphore()
    for dz, dy, dx in FAR_FIRST:
        other = (zs[dz], (ys[dy] + xs[dx]) * 2 + core)
        pl.semaphore_signal(barrier, inc=1, device_id=other, device_id_type=MESH)
    pl.semaphore_signal(barrier, inc=1, device_id=twin, device_id_type=MESH)

    load_start(0).start()
    for c in range(CHUNKS):
        load(c).start()
    load_start(1).start()

    def set_block(x, rows):
        exact[0:rows, :] = x[0:rows]
        h, l = split(x)
        block[0:rows, :LANES] = h
        block[0:rows, LANES:] = l

    def pad_start(i, target):
        load_start(i).wait()
        wide[0:RANK, 0:N] = starts[i]
        target[:, :LANES], target[:, LANES:] = split(wide[...].T)

    def prepare(c):
        rows = pl.ds(c * CHUNK, CHUNK)
        x = staged[c, :, 0:640]
        y = staged[c, :, 640:N]
        high[rows, 0:640], low[rows, 0:640] = split(x)
        high[rows, 640:N], low[rows, 640:N] = split(y)
        x = jnp.sum((x * x).reshape(CHUNK // 8, 8, 640), axis=0)
        y = jnp.sum((y * y).reshape(CHUNK // 8, 8, N - 640), axis=0)
        y = jnp.concatenate([y, jnp.zeros((8, NP - N), F32)], axis=1)
        return sum((x[:, k * LANES : (k + 1) * LANES] for k in range(5)), y)

    def project(c):
        rows = pl.ds(c * CHUNK, CHUNK)
        v = block[...]
        return halves(dot(high[rows, :], v, NN) + dot(low[rows, :], v, NN))

    def product_one():
        total = None
        for c in range(CHUNKS):
            rows = pl.ds(c * CHUNK, CHUNK)
            squares = prepare(c)
            packed[0, 63] = squares if c == 0 else packed[0, 63] + squares
            yh, yl = split(project(c))
            y = jnp.concatenate([yh, yl], axis=1)
            part = tops(dot(y, high[rows, :], NT) + dot(y, low[rows, :], NT))
            total = part if total is None else total + part
        width[...] = total.T

    def gram_block(n, i, right, start):
        rows = slice(i * 256, (i + 1) * 256)
        if n == 0:
            return dot(high[:, rows], right[:, start:], NT)
        return dot(rhigh[rows, :], right[start:, :], TN)

    def gram_copy(n, i):
        part = (n, pl.ds(i * 256, 256), pl.ds(i * 256, NP - i * 256))
        return pltpu.make_async_remote_copy(
            src_ref=gram.at[part],
            dst_ref=gram_in.at[part],
            send_sem=gram_send.at[n, i],
            recv_sem=gram_recv.at[n, i],
            device_id=twin,
            device_id_type=MESH,
        )

    def gram_start(n):
        for i in range(3):
            rows = slice(i * 256, (i + 1) * 256)
            gram[n, rows, i * 256 :] = gram_block(n, i, (high, rhigh)[n], i * 256)
        for i in range(3):
            rows = slice(i * 256, (i + 1) * 256)
            cross_part[rows, :] = gram_block(n, i, (low, rlow)[n], 0)
        for i in range(3):
            for j in range(i, 3):
                a, b = slice(i * 256, (i + 1) * 256), slice(j * 256, (j + 1) * 256)
                gram[n, a, b] = gram[n, a, b] + cross_part[a, b] + cross_part[b, a].T
            gram_copy(n, i).start()

    def gram_pair(n):
        for i in range(3):
            gram_copy(n, i).wait_recv()
            for j in range(i, 3):
                a, b = slice(i * 256, (i + 1) * 256), slice(j * 256, (j + 1) * 256)
                x = gram[n, a, b] + gram_in[n, a, b]
                ghigh[a, b], glow[a, b] = split(x)
                if i != j:
                    ghigh[b, a], glow[b, a] = split(x.T)

    def product_gram():
        v = block[...]
        width[0:N, :] = halves(dot(ghigh[0:N, :], v, NN) + dot(glow[0:N, :], v, NN))

    def product_two():
        v = second[0:N, :]
        z = halves(dot(rhigh[0:N, :], v, NT) + dot(rlow[0:N, :], v, NT))
        zh, zl = split(z)
        zz = jnp.concatenate([zh, zl], axis=1)
        width[0:N, :] = halves(dot(rhigh[0:N, :], zz, NN) + dot(rlow[0:N, :], zz, NN))

    def pack(r):
        tail = width[3 * FOLD : N, :]
        keep = lane((FOLD, LANES)) < RANK
        tiles = FOLD // 8
        for b in range(3):
            body = width[b * FOLD : (b + 1) * FOLD, :]
            moved = pltpu.roll(tail, RANK - 32 * b, 1)
            packed[r, b * tiles : (b + 1) * tiles] = jnp.where(keep, body, moved).reshape(
                tiles, 8, LANES
            )

    def unpack(r):
        if r == 0:
            squares = gathered[0, 63]
            trace = jnp.sum(jnp.sum(squares, axis=1, keepdims=True), axis=0, keepdims=True)
            unit[...] = jnp.broadcast_to(1.0 / trace, (8, LANES))
        scale = unit[0:1, :]
        lanes = lane((FOLD, LANES))
        tiles = FOLD // 8
        tail = jnp.zeros((FOLD, LANES), F32)
        for b in range(3):
            x = gathered[r, b * tiles : (b + 1) * tiles].reshape(FOLD, LANES) * scale
            x0 = jnp.where(lanes < RANK, x, 0.0)
            exact[b * FOLD : (b + 1) * FOLD, :] = x0
            if r % 2 == 0:
                h, l = split(x0)
                block[b * FOLD : (b + 1) * FOLD, :LANES] = h
                block[b * FOLD : (b + 1) * FOLD, LANES:] = l
            moved = pltpu.roll(x, 32 * b + 32, 1)
            tail = jnp.where((lanes >= 32 * b) & (lanes < 32 * b + 32), moved, tail)
        exact[3 * FOLD : N, :] = tail
        if r % 2 == 0:
            h, l = split(tail)
            block[3 * FOLD : N, :LANES] = h
            block[3 * FOLD : N, LANES:] = l

    def send_all(r, src, dst, stage):
        for dz, dy, dx in FAR_FIRST:
            part = ys[dy] + xs[dx]
            pltpu.make_async_remote_copy(
                src_ref=src.at[r, zs[dz] * 16 + part if stage == 0 else chip],
                dst_ref=dst.at[r, chip],
                send_sem=send_sem.at[r, stage],
                recv_sem=recv_sem.at[r, stage],
                device_id=(zs[dz], part * 2 + core),
                device_id_type=MESH,
            ).start()

    def bytes_of(ref, r, sem):
        part = ref.at[r, pl.ds(0, CHIPS - 1)]
        return pltpu.make_async_copy(part, part, sem)

    def reduce_block(r, first=None, last=None):
        pack(r)
        if r == 0:
            pl.semaphore_wait(barrier, CHIPS)
        send_all(r, packed, summed, 0)
        summed[r, pl.ds(chip, 1)] = packed[r, pl.ds(chip, 1)]
        if first is not None:
            first()
        bytes_of(summed, r, recv_sem.at[r, 0]).wait()
        parts = [summed[r, t] for t in range(CHIPS)]
        while len(parts) > 1:
            parts = [a + b for a, b in zip(parts[0::2], parts[1::2])]
        total = parts[0]
        if r % 2 == 0:
            pair[r, pl.ds(core, 1)] = total[None]
            twin_copy = pltpu.make_async_remote_copy(
                src_ref=pair.at[r, core],
                dst_ref=pair.at[r, core],
                send_sem=send_sem.at[r, 1],
                recv_sem=recv_sem.at[r, 1],
                device_id=twin,
                device_id_type=MESH,
            )
            twin_copy.start()
            twin_copy.wait_recv()
            total = pair[r, 0] + pair[r, 1]
        gathered[r, pl.ds(chip, 1)] = total[None]
        send_all(r, gathered, gathered, 2)
        if last is not None:
            last()
        bytes_of(gathered, r, recv_sem.at[r, 2]).wait()
        unpack(r)

    def cross_of():
        v = exact[0:N, :]
        x = lax.dot_general(v, v, NT, precision=lax.Precision.HIGHEST, preferred_element_type=F32)
        upper[...] = x[0:RANK, :]
        rows = lax.broadcasted_iota(jnp.int32, (RANK, LANES), 0)
        lower[...] = jnp.where(rows == lane((RANK, LANES)), 1.0, 0.0)

    def panel(p, tiles):
        start = pl.multiple_of(8 * p, 8)
        u = upper[pl.ds(start, 8), :]
        w = lower[pl.ds(start, 8), :]
        sub = lax.broadcasted_iota(jnp.int32, (8, LANES), 0)
        full = (8, LANES)
        cols = [jnp.broadcast_to(u[:, j : j + 1], full) for j in range(8)]
        urow, wrow, inv, elem = [], [], [], {}
        pivots = jnp.ones(full, F32)
        for j in range(8):
            pivot = jnp.broadcast_to(cols[j][j : j + 1, :], full)
            inv.append(1.0 / pivot)
            pivots = jnp.where(sub == j, pivot, pivots)
            factor = jnp.where(sub > j, cols[j] * inv[j], 0.0)
            urow.append(jnp.broadcast_to(u[j : j + 1, :], full))
            wrow.append(jnp.broadcast_to(w[j : j + 1, :], full))
            u = u - factor * urow[j]
            w = w - factor * wrow[j]
            for k in range(j + 1, 8):
                elem[j, k] = jnp.broadcast_to(cols[k][j : j + 1, :], full)
                cols[k] = cols[k] - factor * elem[j, k]
        inverse[pl.ds(start, 8), :] = w * lax.rsqrt(pivots)
        for t in tiles:
            u = upper[8 * t : 8 * t + 8, :]
            w = lower[8 * t : 8 * t + 8, :]
            cols = [jnp.broadcast_to(u[:, j : j + 1], full) for j in range(8)]
            for j in range(8):
                factor = cols[j] * inv[j]
                u = u - factor * urow[j]
                w = w - factor * wrow[j]
                for k in range(j + 1, 8):
                    cols[k] = cols[k] - factor * elem[j, k]
            upper[8 * t : 8 * t + 8, :] = pltpu.roll(u, LANES - 8, 1)
            lower[8 * t : 8 * t + 8, :] = w

    def panels(first, last):
        def step(p, carry):
            panel(p, range(first + 1, 12))
            return carry

        lax.fori_loop(first, last, step, 0)

    def stack():
        h, l = split(inverse[...])
        stacked[:LANES, :] = h
        stacked[LANES:, :] = l

    def factor_start():
        cross_of()
        panels(0, 4)

    def factor_end():
        panels(4, 8)
        panels(8, 12)

    def basis():
        return lax.dot_general(
            inverse[0:RANK, :], exact[0:N, :], TN,
            precision=lax.Precision.HIGHEST, preferred_element_type=F32,
        )

    def apply(rows):
        return lax.dot_general(exact[rows, :], inverse[...], TN, precision=lax.Precision.HIGHEST, preferred_element_type=F32)

    def first_window():
        factor_start()
        pad_start(1, second)

    def third_window():
        gram_pair(1)
        out_one[...] = basis()

    packed[1:, 63] = jnp.zeros((3, 8, LANES), F32)
    high[:, 640:NP] = jnp.zeros((high.shape[0], LANES), BF16)
    low[:, 640:NP] = jnp.zeros((low.shape[0], LANES), BF16)
    inverse[...] = jnp.zeros_like(inverse)
    rhigh[N:NP, :] = jnp.zeros((NP - N, 2 * LANES), BF16)
    rlow[N:NP, :] = jnp.zeros((NP - N, 2 * LANES), BF16)
    wide[...] = jnp.zeros_like(wide)
    pad_start(0, block)
    for c in range(CHUNKS):
        load(c).wait()
    product_one()
    reduce_block(0, lambda: gram_start(0), lambda: gram_pair(0))
    product_gram()
    reduce_block(1, first_window, factor_end)
    set_block(apply(slice(0, N)), N)

    def fold(target, body, tail):
        keep = lane((tail, LANES)) < RANK
        end = line[body : body + tail, :]
        for b in range(3):
            rows = slice(b * tail, (b + 1) * tail)
            target[rows] = jnp.where(keep, line[rows, :], pltpu.roll(end, RANK - 32 * b, 1))
        if body > 3 * tail:
            target[3 * tail : body] = line[3 * tail : body, :]

    def unfold(source, start, body, tail):
        lanes = lane((tail, LANES))
        end = jnp.zeros((tail, LANES), F32)
        for b in range(3):
            x = source[b * tail : (b + 1) * tail]
            line[start + b * tail : start + (b + 1) * tail, :] = jnp.where(lanes < RANK, x, 0.0)
            inside = (lanes >= 32 * b) & (lanes < 32 * b + 32)
            end = jnp.where(inside, pltpu.roll(x, 32 * b + 32, 1), end)
        if body > 3 * tail:
            line[start + 3 * tail : start + body, :] = source[3 * tail : body]
        line[start + body : start + body + tail, :] = end

    def swap(src, dst, k, r):
        g = lax.rem(grp + k, GRP)
        return pltpu.make_async_remote_copy(
            src_ref=src(g),
            dst_ref=dst,
            send_sem=swap_send.at[r],
            recv_sem=swap_recv.at[r],
            device_id=(g, slab),
            device_id_type=MESH,
        )

    def three(ref, sem):
        part = ref.at[pl.ds(0, GRP - 1)]
        return pltpu.make_async_copy(part, part, sem)

    for c in range(CHUNKS):
        rtilde[c * CHUNK : (c + 1) * CHUNK, :] = project(c)
        for g in range(GRP):
            for m in range(2):
                line[m * STEP : (m + 1) * STEP, :] = rtilde[
                    pl.ds(c * CHUNK + 2 * g + m, STEP, stride=COLS), :
                ]
            fold(mode.at[c, g], BODY, TAIL)
        for k in (2, 1, 3):
            swap(lambda g: mode.at[c, g], given.at[c, grp], k, c).start()
        given[c, pl.ds(grp, 1)] = mode[c, pl.ds(grp, 1)]
    factor_start()
    factor_end()
    stack()
    f = stacked[...]
    for c in range(CHUNKS):
        three(given.at[c], swap_recv.at[c]).wait()
        size = 2 * STEP
        for g in range(GRP):
            unfold(given.at[c, g], g * size, BODY, TAIL)
        h, l = split(line[...])
        y = halves(dot(h, f, TN) + dot(l, f, TN))
        for g in range(GRP):
            rows = slice(g * ROWS + c * STEP, g * ROWS + (c + 1) * STEP)
            for m in range(2):
                h, l = split(y[g * size + m * STEP : g * size + (m + 1) * STEP])
                rhigh[rows, m * LANES : (m + 1) * LANES] = h
                rlow[rows, m * LANES : (m + 1) * LANES] = l
    for c in range(CHUNKS):
        three(mode.at[c], swap_send.at[c]).wait()

    product_two()
    reduce_block(2, lambda: gram_start(1), third_window)
    product_gram()
    reduce_block(3, factor_start, factor_end)
    set_block(apply(slice(0, N)), N)
    v = block[0:N, :]
    partial = tops(dot(v, rhigh[0:N, :], NT) + dot(v, rlow[0:N, :], NT))
    for m in range(2):
        line[m * RANK : (m + 1) * RANK, :] = partial[0:RANK, m * LANES : (m + 1) * LANES]
    fold(core_out, CORE_BODY, CORE_TAIL)
    for k in (2, 1, 3):
        swap(lambda g: core_out, core_in.at[grp], k, CHUNKS).start()
    core_in[pl.ds(grp, 1)] = core_out[...][None]
    factor_start()
    factor_end()
    out_two[...] = basis()
    mine = inverse[pl.ds(pl.multiple_of(grp * 24, 8), 24), 0:RANK]
    three(core_in, swap_recv.at[CHUNKS]).wait()
    for g in range(GRP):
        unfold(core_in.at[g], 0, CORE_BODY, CORE_TAIL)
        x = jnp.concatenate([line[0:RANK, :], line[RANK : 2 * RANK, :]], axis=1)
        y = jnp.dot(mine, x, precision=lax.Precision.HIGHEST)
        for m in range(2):
            out_core[pl.ds(2 * g + m, 24, stride=COLS), :] = y[:, m * LANES : m * LANES + RANK]
    for k in range(1, GRP):
        pltpu.make_async_copy(core_out, core_out, swap_send.at[CHUNKS]).wait()
    for i in range(3):
        gram_copy(0, i).wait_send()
        gram_copy(1, i).wait_send()
    for r in range(4):
        bytes_of(packed, r, send_sem.at[r, 0]).wait()
        if r % 2 == 0:
            pltpu.make_async_copy(pair.at[r, 0], pair.at[r, 0], send_sem.at[r, 1]).wait()
        bytes_of(gathered, r, send_sem.at[r, 2]).wait()


def finish(one, two, core, out_one, out_two, out_core, sems):
    pairs = ((one, out_one), (two, out_two), (core, out_core))
    copies = [pltpu.make_async_copy(a, b, sems.at[i]) for i, (a, b) in enumerate(pairs)]
    for copy in copies:
        copy.start()
    for copy in copies:
        copy.wait()


def local(tensor, start_one, start_two):
    rows = ROWS * COLS
    vmem = pl.BlockSpec(memory_space=pltpu.VMEM)
    hbm = pl.BlockSpec(memory_space=pltpu.HBM)
    basis_one, basis_two, core = pl.pallas_call(
        kernel,
        out_shape=(
            jax.ShapeDtypeStruct((RANK, N), F32),
            jax.ShapeDtypeStruct((RANK, N), F32),
            jax.ShapeDtypeStruct((RANK // GRP * COLS, RANK), F32),
        ),
        in_specs=[hbm, hbm, hbm],
        out_specs=(vmem, vmem, vmem),
        scratch_shapes=[
            pltpu.VMEM((CHUNKS, CHUNK, N), F32),
            pltpu.VMEM((2, RANK, N), F32),
            pltpu.VMEM((LANES, NP), F32),
            pltpu.VMEM((NP, 2 * LANES), BF16),
            pltpu.VMEM((2, NP, NP), F32),
            pltpu.VMEM((2, NP, NP), F32),
            pltpu.VMEM((NP, NP), F32),
            pltpu.VMEM((NP, NP), BF16),
            pltpu.VMEM((NP, NP), BF16),
            pltpu.VMEM((rows, NP), BF16),
            pltpu.VMEM((rows, NP), BF16),
            pltpu.VMEM((NP, 2 * LANES), BF16),
            pltpu.VMEM((NP, LANES), F32),
            pltpu.VMEM((NP, LANES), F32),
            pltpu.VMEM((NP, 2 * LANES), BF16),
            pltpu.VMEM((NP, 2 * LANES), BF16),
            pltpu.VMEM((rows, LANES), F32),
            pltpu.VMEM((CHUNK, LANES), F32),
            pltpu.VMEM((CHUNKS, GRP, BODY, LANES), F32),
            pltpu.VMEM((CHUNKS, GRP, BODY, LANES), F32),
            pltpu.VMEM((4, CHIPS, 8, LANES), F32),
            pltpu.VMEM((4, CHIPS, 8, LANES), F32),
            pltpu.VMEM((4, 2, 8, LANES), F32),
            pltpu.VMEM((4, CHIPS, 8, LANES), F32),
            pltpu.VMEM((CORE_BODY, LANES), F32),
            pltpu.VMEM((GRP, CORE_BODY, LANES), F32),
            pltpu.VMEM((8, LANES), F32),
            pltpu.VMEM((RANK, LANES), F32),
            pltpu.VMEM((RANK, LANES), F32),
            pltpu.VMEM((LANES, LANES), F32),
            pltpu.VMEM((2 * LANES, LANES), BF16),
            pltpu.SemaphoreType.DMA((CHUNKS + 2,)),
            pltpu.SemaphoreType.DMA((4, 3)),
            pltpu.SemaphoreType.DMA((4, 3)),
            pltpu.SemaphoreType.DMA((CHUNKS + 1,)),
            pltpu.SemaphoreType.DMA((CHUNKS + 1,)),
            pltpu.SemaphoreType.DMA((2, 3)),
            pltpu.SemaphoreType.DMA((2, 3)),
        ],
        compiler_params=pltpu.CompilerParams(
            collective_id=0, has_side_effects=True, vmem_limit_bytes=48 << 20
        ),
    )(
        pltpu.with_memory_space_constraint(tensor.reshape(rows, N), pltpu.HBM),
        pltpu.with_memory_space_constraint(start_one.T, pltpu.HBM),
        pltpu.with_memory_space_constraint(start_two.T, pltpu.HBM),
    )
    basis_one, basis_two, core = pl.pallas_call(
        finish,
        out_shape=(
            jax.ShapeDtypeStruct((RANK, N), F32),
            jax.ShapeDtypeStruct((RANK, N), F32),
            jax.ShapeDtypeStruct((RANK // GRP * COLS, RANK), F32),
        ),
        in_specs=[vmem, vmem, vmem],
        out_specs=(hbm, hbm, hbm),
        scratch_shapes=[pltpu.SemaphoreType.DMA((3,))],
    )(*(pltpu.with_memory_space_constraint(x, pltpu.VMEM) for x in (basis_one, basis_two, core)))
    return basis_one.T, basis_two.T, core.reshape(RANK // GRP, COLS, RANK)


def solution(mesh):
    in_specs = (P("grp", "slab", None), P(), P())
    out_specs = (P(), P(), P("grp", "slab", None))
    return jax.shard_map(local, mesh=mesh, in_specs=in_specs, out_specs=out_specs, check_vma=False)
```

```python
import jax
import jax.numpy as jnp
from jax import lax
from jax.experimental import pallas as pl
from jax.experimental.pallas import tpu as pltpu
from jax.sharding import PartitionSpec as P

MESH = pl.DeviceIdType.MESH
F32 = jnp.float32
BF16 = jnp.bfloat16

N = 672
NP = 768
RANK = 96
LANES = 128
GRP = 4
COLS = 8
ROWS = N // GRP
CHUNK = 448
CHUNKS = ROWS * COLS // CHUNK
CHIPS = 64
STEP = CHUNK // COLS
BODY, TAIL = 88, 24
CORE_BODY, CORE_TAIL = 144, 48
FOLD = N // 4
OFFSETS = [(z, y, x) for z in range(4) for y in range(4) for x in range(4)]
FAR_FIRST = sorted(OFFSETS[1:], key=lambda o: -sum(min(d, 4 - d) for d in o))
NT = (((0,), (0,)), ((), ()))
NN = (((1,), (0,)), ((), ()))
TN = (((1,), (1,)), ((), ()))


def dot(a, b, dims):
    return lax.dot_general(a, b, dims, preferred_element_type=F32)


def split(x):
    high = x.astype(BF16)
    return high, (x - high.astype(F32)).astype(BF16)


def halves(x):
    return x[:, :LANES] + x[:, LANES:]


def tops(x):
    return x[:LANES] + x[LANES:]


def lane(shape):
    return lax.broadcasted_iota(jnp.int32, shape, len(shape) - 1)


def kernel(
    tensor, start_one, start_two, out_one, out_two, out_core,
    staged, starts, wide, second, gram, gram_in, cross_part, ghigh, glow, high, low, block, exact, width, rhigh, rlow, rtilde, line, mode, given,
    packed, summed, pair, gathered, core_out, core_in,
    unit, upper, lower, inverse, stacked,
    load_sem, send_sem, recv_sem, swap_send, swap_recv, gram_send, gram_recv,
):
    grp = lax.axis_index("grp")
    slab = lax.axis_index("slab")
    core = lax.rem(slab, 2)
    chip = grp * 16 + slab // 2

    zs = [grp] + [lax.rem(grp + d, 4) for d in range(1, 4)]
    ys = [lax.rem(slab // 8 + d, 4) * 4 for d in range(4)]
    xs = [lax.rem(slab // 2 + d, 4) for d in range(4)]
    twin = (grp, slab + 1 - 2 * core)

    def load(c):
        return pltpu.make_async_copy(
            tensor.at[pl.ds(c * CHUNK, CHUNK)], staged.at[c], load_sem.at[c]
        )

    def load_start(i):
        return pltpu.make_async_copy(
            (start_one, start_two)[i], starts.at[i], load_sem.at[CHUNKS + i]
        )

    barrier = pltpu.get_barrier_semaphore()
    for dz, dy, dx in FAR_FIRST:
        other = (zs[dz], (ys[dy] + xs[dx]) * 2 + core)
        pl.semaphore_signal(barrier, inc=1, device_id=other, device_id_type=MESH)
    pl.semaphore_signal(barrier, inc=1, device_id=twin, device_id_type=MESH)

    load_start(0).start()
    for c in range(CHUNKS):
        load(c).start()
    load_start(1).start()

    def set_block(x, rows):
        exact[0:rows, :] = x[0:rows]
        h, l = split(x)
        block[0:rows, :LANES] = h
        block[0:rows, LANES:] = l

    def pad_start(i, target):
        load_start(i).wait()
        wide[0:RANK, 0:N] = starts[i]
        target[:, :LANES], target[:, LANES:] = split(wide[...].T)

    def prepare(c):
        rows = pl.ds(c * CHUNK, CHUNK)
        x = staged[c, :, 0:640]
        y = staged[c, :, 640:N]
        high[rows, 0:640], low[rows, 0:640] = split(x)
        high[rows, 640:N], low[rows, 640:N] = split(y)
        x = jnp.sum((x * x).reshape(CHUNK // 8, 8, 640), axis=0)
        y = jnp.sum((y * y).reshape(CHUNK // 8, 8, N - 640), axis=0)
        y = jnp.concatenate([y, jnp.zeros((8, NP - N), F32)], axis=1)
        return sum((x[:, k * LANES : (k + 1) * LANES] for k in range(5)), y)

    def project(c):
        rows = pl.ds(c * CHUNK, CHUNK)
        v = block[...]
        return halves(dot(high[rows, :], v, NN) + dot(low[rows, :], v, NN))

    def product_one():
        total = None
        for c in range(CHUNKS):
            rows = pl.ds(c * CHUNK, CHUNK)
            squares = prepare(c)
            packed[0, 63] = squares if c == 0 else packed[0, 63] + squares
            yh, yl = split(project(c))
            y = jnp.concatenate([yh, yl], axis=1)
            part = tops(dot(y, high[rows, :], NT) + dot(y, low[rows, :], NT))
            total = part if total is None else total + part
        width[...] = total.T

    def gram_block(n, i, right, start):
        rows = slice(i * 256, (i + 1) * 256)
        if n == 0:
            return dot(high[:, rows], right[:, start:], NT)
        return dot(rhigh[rows, :], right[start:, :], TN)

    def gram_copy(n, i):
        part = (n, pl.ds(i * 256, 256), pl.ds(i * 256, NP - i * 256))
        return pltpu.make_async_remote_copy(
            src_ref=gram.at[part],
            dst_ref=gram_in.at[part],
            send_sem=gram_send.at[n, i],
            recv_sem=gram_recv.at[n, i],
            device_id=twin,
            device_id_type=MESH,
        )

    def gram_start(n):
        for i in range(3):
            rows = slice(i * 256, (i + 1) * 256)
            gram[n, rows, i * 256 :] = gram_block(n, i, (high, rhigh)[n], i * 256)
        for i in range(3):
            rows = slice(i * 256, (i + 1) * 256)
            cross_part[rows, :] = gram_block(n, i, (low, rlow)[n], 0)
        for i in range(3):
            for j in range(i, 3):
                a, b = slice(i * 256, (i + 1) * 256), slice(j * 256, (j + 1) * 256)
                gram[n, a, b] = gram[n, a, b] + cross_part[a, b] + cross_part[b, a].T
            gram_copy(n, i).start()

    def gram_pair(n):
        for i in range(3):
            gram_copy(n, i).wait_recv()
            for j in range(i, 3):
                a, b = slice(i * 256, (i + 1) * 256), slice(j * 256, (j + 1) * 256)
                x = gram[n, a, b] + gram_in[n, a, b]
                ghigh[a, b], glow[a, b] = split(x)
                if i != j:
                    ghigh[b, a], glow[b, a] = split(x.T)

    def product_gram():
        v = block[...]
        width[0:N, :] = halves(dot(ghigh[0:N, :], v, NN) + dot(glow[0:N, :], v, NN))

    def product_two():
        v = second[0:N, :]
        z = halves(dot(rhigh[0:N, :], v, NT) + dot(rlow[0:N, :], v, NT))
        zh, zl = split(z)
        zz = jnp.concatenate([zh, zl], axis=1)
        width[0:N, :] = halves(dot(rhigh[0:N, :], zz, NN) + dot(rlow[0:N, :], zz, NN))

    def pack(r):
        tail = width[3 * FOLD : N, :]
        keep = lane((FOLD, LANES)) < RANK
        tiles = FOLD // 8
        for b in range(3):
            body = width[b * FOLD : (b + 1) * FOLD, :]
            moved = pltpu.roll(tail, RANK - 32 * b, 1)
            packed[r, b * tiles : (b + 1) * tiles] = jnp.where(keep, body, moved).reshape(
                tiles, 8, LANES
            )

    def unpack(r):
        if r == 0:
            squares = gathered[0, 63]
            trace = jnp.sum(jnp.sum(squares, axis=1, keepdims=True), axis=0, keepdims=True)
            unit[...] = jnp.broadcast_to(1.0 / trace, (8, LANES))
        scale = unit[0:1, :]
        lanes = lane((FOLD, LANES))
        tiles = FOLD // 8
        tail = jnp.zeros((FOLD, LANES), F32)
        for b in range(3):
            x = gathered[r, b * tiles : (b + 1) * tiles].reshape(FOLD, LANES) * scale
            x0 = jnp.where(lanes < RANK, x, 0.0)
            exact[b * FOLD : (b + 1) * FOLD, :] = x0
            if r % 2 == 0:
                h, l = split(x0)
                block[b * FOLD : (b + 1) * FOLD, :LANES] = h
                block[b * FOLD : (b + 1) * FOLD, LANES:] = l
            moved = pltpu.roll(x, 32 * b + 32, 1)
            tail = jnp.where((lanes >= 32 * b) & (lanes < 32 * b + 32), moved, tail)
        exact[3 * FOLD : N, :] = tail
        if r % 2 == 0:
            h, l = split(tail)
            block[3 * FOLD : N, :LANES] = h
            block[3 * FOLD : N, LANES:] = l

    def send_all(r, src, dst, stage):
        for dz, dy, dx in FAR_FIRST:
            part = ys[dy] + xs[dx]
            pltpu.make_async_remote_copy(
                src_ref=src.at[r, zs[dz] * 16 + part if stage == 0 else chip],
                dst_ref=dst.at[r, chip],
                send_sem=send_sem.at[r, stage],
                recv_sem=recv_sem.at[r, stage],
                device_id=(zs[dz], part * 2 + core),
                device_id_type=MESH,
            ).start()

    def bytes_of(ref, r, sem):
        part = ref.at[r, pl.ds(0, CHIPS - 1)]
        return pltpu.make_async_copy(part, part, sem)

    def reduce_block(r, first=None, last=None):
        pack(r)
        if r == 0:
            pl.semaphore_wait(barrier, CHIPS)
        send_all(r, packed, summed, 0)
        summed[r, pl.ds(chip, 1)] = packed[r, pl.ds(chip, 1)]
        if first is not None:
            first()
        bytes_of(summed, r, recv_sem.at[r, 0]).wait()
        parts = [summed[r, t] for t in range(CHIPS)]
        while len(parts) > 1:
            parts = [a + b for a, b in zip(parts[0::2], parts[1::2])]
        total = parts[0]
        if r % 2 == 0:
            pair[r, pl.ds(core, 1)] = total[None]
            twin_copy = pltpu.make_async_remote_copy(
                src_ref=pair.at[r, core],
                dst_ref=pair.at[r, core],
                send_sem=send_sem.at[r, 1],
                recv_sem=recv_sem.at[r, 1],
                device_id=twin,
                device_id_type=MESH,
            )
            twin_copy.start()
            twin_copy.wait_recv()
            total = pair[r, 0] + pair[r, 1]
        gathered[r, pl.ds(chip, 1)] = total[None]
        send_all(r, gathered, gathered, 2)
        if last is not None:
            last()
        bytes_of(gathered, r, recv_sem.at[r, 2]).wait()
        unpack(r)

    def cross_of():
        v = exact[0:N, :]
        x = lax.dot_general(v, v, NT, precision=lax.Precision.HIGHEST, preferred_element_type=F32)
        upper[...] = x[0:RANK, :]
        rows = lax.broadcasted_iota(jnp.int32, (RANK, LANES), 0)
        lower[...] = jnp.where(rows == lane((RANK, LANES)), 1.0, 0.0)

    def panel(p, tiles):
        start = pl.multiple_of(8 * p, 8)
        u = upper[pl.ds(start, 8), :]
        w = lower[pl.ds(start, 8), :]
        sub = lax.broadcasted_iota(jnp.int32, (8, LANES), 0)
        full = (8, LANES)
        cols = [jnp.broadcast_to(u[:, j : j + 1], full) for j in range(8)]
        urow, wrow, inv, elem = [], [], [], {}
        pivots = jnp.ones(full, F32)
        for j in range(8):
            pivot = jnp.broadcast_to(cols[j][j : j + 1, :], full)
            inv.append(1.0 / pivot)
            pivots = jnp.where(sub == j, pivot, pivots)
            factor = jnp.where(sub > j, cols[j] * inv[j], 0.0)
            urow.append(jnp.broadcast_to(u[j : j + 1, :], full))
            wrow.append(jnp.broadcast_to(w[j : j + 1, :], full))
            u = u - factor * urow[j]
            w = w - factor * wrow[j]
            for k in range(j + 1, 8):
                elem[j, k] = jnp.broadcast_to(cols[k][j : j + 1, :], full)
                cols[k] = cols[k] - factor * elem[j, k]
        inverse[pl.ds(start, 8), :] = w * lax.rsqrt(pivots)
        for t in tiles:
            u = upper[8 * t : 8 * t + 8, :]
            w = lower[8 * t : 8 * t + 8, :]
            cols = [jnp.broadcast_to(u[:, j : j + 1], full) for j in range(8)]
            for j in range(8):
                factor = cols[j] * inv[j]
                u = u - factor * urow[j]
                w = w - factor * wrow[j]
                for k in range(j + 1, 8):
                    cols[k] = cols[k] - factor * elem[j, k]
            upper[8 * t : 8 * t + 8, :] = pltpu.roll(u, LANES - 8, 1)
            lower[8 * t : 8 * t + 8, :] = w

    def panels(first, last):
        def step(p, carry):
            panel(p, range(first + 1, 12))
            return carry

        lax.fori_loop(first, last, step, 0)

    def stack():
        h, l = split(inverse[...])
        stacked[:LANES, :] = h
        stacked[LANES:, :] = l

    def factor_start():
        cross_of()
        panels(0, 4)

    def factor_end():
        panels(4, 8)
        panels(8, 12)

    def basis():
        return lax.dot_general(
            inverse[0:RANK, :], exact[0:N, :], TN,
            precision=lax.Precision.HIGHEST, preferred_element_type=F32,
        )

    def apply(rows):
        x = exact[rows, :]
        high_x, mid_x = split(x)
        low_x = (x - high_x.astype(F32) - mid_x.astype(F32)).astype(BF16)
        f = inverse[...]
        high_f, mid_f = split(f)
        low_f = (f - high_f.astype(F32) - mid_f.astype(F32)).astype(BF16)
        two = jnp.concatenate([high_f, mid_f], axis=0)
        main = halves(dot(high_x, two, TN) + dot(mid_x, two, TN))
        return main + (dot(high_x, low_f, TN) + dot(low_x, high_f, TN))

    def first_window():
        factor_start()
        pad_start(1, second)

    def third_window():
        gram_pair(1)
        out_one[...] = basis()

    packed[1:, 63] = jnp.zeros((3, 8, LANES), F32)
    high[:, 640:NP] = jnp.zeros((high.shape[0], LANES), BF16)
    low[:, 640:NP] = jnp.zeros((low.shape[0], LANES), BF16)
    inverse[...] = jnp.zeros_like(inverse)
    rhigh[N:NP, :] = jnp.zeros((NP - N, 2 * LANES), BF16)
    rlow[N:NP, :] = jnp.zeros((NP - N, 2 * LANES), BF16)
    wide[...] = jnp.zeros_like(wide)
    pad_start(0, block)
    for c in range(CHUNKS):
        load(c).wait()
    product_one()
    reduce_block(0, lambda: gram_start(0), lambda: gram_pair(0))
    product_gram()
    reduce_block(1, first_window, factor_end)
    set_block(apply(slice(0, N)), N)

    def fold(target, body, tail):
        keep = lane((tail, LANES)) < RANK
        end = line[body : body + tail, :]
        for b in range(3):
            rows = slice(b * tail, (b + 1) * tail)
            target[rows] = jnp.where(keep, line[rows, :], pltpu.roll(end, RANK - 32 * b, 1))
        if body > 3 * tail:
            target[3 * tail : body] = line[3 * tail : body, :]

    def unfold(source, start, body, tail):
        lanes = lane((tail, LANES))
        end = jnp.zeros((tail, LANES), F32)
        for b in range(3):
            x = source[b * tail : (b + 1) * tail]
            line[start + b * tail : start + (b + 1) * tail, :] = jnp.where(lanes < RANK, x, 0.0)
            inside = (lanes >= 32 * b) & (lanes < 32 * b + 32)
            end = jnp.where(inside, pltpu.roll(x, 32 * b + 32, 1), end)
        if body > 3 * tail:
            line[start + 3 * tail : start + body, :] = source[3 * tail : body]
        line[start + body : start + body + tail, :] = end

    def swap(src, dst, k, r):
        g = lax.rem(grp + k, GRP)
        return pltpu.make_async_remote_copy(
            src_ref=src(g),
            dst_ref=dst,
            send_sem=swap_send.at[r],
            recv_sem=swap_recv.at[r],
            device_id=(g, slab),
            device_id_type=MESH,
        )

    def three(ref, sem):
        part = ref.at[pl.ds(0, GRP - 1)]
        return pltpu.make_async_copy(part, part, sem)

    for c in range(CHUNKS):
        rtilde[c * CHUNK : (c + 1) * CHUNK, :] = project(c)
        for g in range(GRP):
            for m in range(2):
                line[m * STEP : (m + 1) * STEP, :] = rtilde[
                    pl.ds(c * CHUNK + 2 * g + m, STEP, stride=COLS), :
                ]
            fold(mode.at[c, g], BODY, TAIL)
        for k in (2, 1, 3):
            swap(lambda g: mode.at[c, g], given.at[c, grp], k, c).start()
        given[c, pl.ds(grp, 1)] = mode[c, pl.ds(grp, 1)]
    factor_start()
    factor_end()
    stack()
    f = stacked[...]
    for c in range(CHUNKS):
        three(given.at[c], swap_recv.at[c]).wait()
        size = 2 * STEP
        for g in range(GRP):
            unfold(given.at[c, g], g * size, BODY, TAIL)
        h, l = split(line[...])
        y = halves(dot(h, f, TN) + dot(l, f, TN))
        for g in range(GRP):
            rows = slice(g * ROWS + c * STEP, g * ROWS + (c + 1) * STEP)
            for m in range(2):
                h, l = split(y[g * size + m * STEP : g * size + (m + 1) * STEP])
                rhigh[rows, m * LANES : (m + 1) * LANES] = h
                rlow[rows, m * LANES : (m + 1) * LANES] = l
    for c in range(CHUNKS):
        three(mode.at[c], swap_send.at[c]).wait()

    product_two()
    reduce_block(2, lambda: gram_start(1), third_window)
    product_gram()
    reduce_block(3, factor_start, factor_end)
    set_block(apply(slice(0, N)), N)
    v = block[0:N, :]
    partial = tops(dot(v, rhigh[0:N, :], NT) + dot(v, rlow[0:N, :], NT))
    for m in range(2):
        line[m * RANK : (m + 1) * RANK, :] = partial[0:RANK, m * LANES : (m + 1) * LANES]
    fold(core_out, CORE_BODY, CORE_TAIL)
    for k in (2, 1, 3):
        swap(lambda g: core_out, core_in.at[grp], k, CHUNKS).start()
    core_in[pl.ds(grp, 1)] = core_out[...][None]
    factor_start()
    factor_end()
    out_two[...] = basis()
    mine = inverse[pl.ds(pl.multiple_of(grp * 24, 8), 24), 0:RANK]
    three(core_in, swap_recv.at[CHUNKS]).wait()
    for g in range(GRP):
        unfold(core_in.at[g], 0, CORE_BODY, CORE_TAIL)
        x = jnp.concatenate([line[0:RANK, :], line[RANK : 2 * RANK, :]], axis=1)
        y = jnp.dot(mine, x, precision=lax.Precision.HIGHEST)
        for m in range(2):
            out_core[pl.ds(2 * g + m, 24, stride=COLS), :] = y[:, m * LANES : m * LANES + RANK]
    for k in range(1, GRP):
        pltpu.make_async_copy(core_out, core_out, swap_send.at[CHUNKS]).wait()
    for i in range(3):
        gram_copy(0, i).wait_send()
        gram_copy(1, i).wait_send()
    for r in range(4):
        bytes_of(packed, r, send_sem.at[r, 0]).wait()
        if r % 2 == 0:
            pltpu.make_async_copy(pair.at[r, 0], pair.at[r, 0], send_sem.at[r, 1]).wait()
        bytes_of(gathered, r, send_sem.at[r, 2]).wait()


def finish(one, two, core, out_one, out_two, out_core, sems):
    pairs = ((one, out_one), (two, out_two), (core, out_core))
    copies = [pltpu.make_async_copy(a, b, sems.at[i]) for i, (a, b) in enumerate(pairs)]
    for copy in copies:
        copy.start()
    for copy in copies:
        copy.wait()


def local(tensor, start_one, start_two):
    rows = ROWS * COLS
    vmem = pl.BlockSpec(memory_space=pltpu.VMEM)
    hbm = pl.BlockSpec(memory_space=pltpu.HBM)
    basis_one, basis_two, core = pl.pallas_call(
        kernel,
        out_shape=(
            jax.ShapeDtypeStruct((RANK, N), F32),
            jax.ShapeDtypeStruct((RANK, N), F32),
            jax.ShapeDtypeStruct((RANK // GRP * COLS, RANK), F32),
        ),
        in_specs=[hbm, hbm, hbm],
        out_specs=(vmem, vmem, vmem),
        scratch_shapes=[
            pltpu.VMEM((CHUNKS, CHUNK, N), F32),
            pltpu.VMEM((2, RANK, N), F32),
            pltpu.VMEM((LANES, NP), F32),
            pltpu.VMEM((NP, 2 * LANES), BF16),
            pltpu.VMEM((2, NP, NP), F32),
            pltpu.VMEM((2, NP, NP), F32),
            pltpu.VMEM((NP, NP), F32),
            pltpu.VMEM((NP, NP), BF16),
            pltpu.VMEM((NP, NP), BF16),
            pltpu.VMEM((rows, NP), BF16),
            pltpu.VMEM((rows, NP), BF16),
            pltpu.VMEM((NP, 2 * LANES), BF16),
            pltpu.VMEM((NP, LANES), F32),
            pltpu.VMEM((NP, LANES), F32),
            pltpu.VMEM((NP, 2 * LANES), BF16),
            pltpu.VMEM((NP, 2 * LANES), BF16),
            pltpu.VMEM((rows, LANES), F32),
            pltpu.VMEM((CHUNK, LANES), F32),
            pltpu.VMEM((CHUNKS, GRP, BODY, LANES), F32),
            pltpu.VMEM((CHUNKS, GRP, BODY, LANES), F32),
            pltpu.VMEM((4, CHIPS, 8, LANES), F32),
            pltpu.VMEM((4, CHIPS, 8, LANES), F32),
            pltpu.VMEM((4, 2, 8, LANES), F32),
            pltpu.VMEM((4, CHIPS, 8, LANES), F32),
            pltpu.VMEM((CORE_BODY, LANES), F32),
            pltpu.VMEM((GRP, CORE_BODY, LANES), F32),
            pltpu.VMEM((8, LANES), F32),
            pltpu.VMEM((RANK, LANES), F32),
            pltpu.VMEM((RANK, LANES), F32),
            pltpu.VMEM((LANES, LANES), F32),
            pltpu.VMEM((2 * LANES, LANES), BF16),
            pltpu.SemaphoreType.DMA((CHUNKS + 2,)),
            pltpu.SemaphoreType.DMA((4, 3)),
            pltpu.SemaphoreType.DMA((4, 3)),
            pltpu.SemaphoreType.DMA((CHUNKS + 1,)),
            pltpu.SemaphoreType.DMA((CHUNKS + 1,)),
            pltpu.SemaphoreType.DMA((2, 3)),
            pltpu.SemaphoreType.DMA((2, 3)),
        ],
        compiler_params=pltpu.CompilerParams(
            collective_id=0, has_side_effects=True, vmem_limit_bytes=48 << 20
        ),
    )(
        pltpu.with_memory_space_constraint(tensor.reshape(rows, N), pltpu.HBM),
        pltpu.with_memory_space_constraint(start_one.T, pltpu.HBM),
        pltpu.with_memory_space_constraint(start_two.T, pltpu.HBM),
    )
    basis_one, basis_two, core = pl.pallas_call(
        finish,
        out_shape=(
            jax.ShapeDtypeStruct((RANK, N), F32),
            jax.ShapeDtypeStruct((RANK, N), F32),
            jax.ShapeDtypeStruct((RANK // GRP * COLS, RANK), F32),
        ),
        in_specs=[vmem, vmem, vmem],
        out_specs=(hbm, hbm, hbm),
        scratch_shapes=[pltpu.SemaphoreType.DMA((3,))],
    )(*(pltpu.with_memory_space_constraint(x, pltpu.VMEM) for x in (basis_one, basis_two, core)))
    return basis_one.T, basis_two.T, core.reshape(RANK // GRP, COLS, RANK)


def solution(mesh):
    in_specs = (P("grp", "slab", None), P(), P())
    out_specs = (P(), P(), P("grp", "slab", None))
    return jax.shard_map(local, mesh=mesh, in_specs=in_specs, out_specs=out_specs, check_vma=False)
```
